32 devices in a mesh: grp: 4 (over x, core), fsdp: 8 (over z, y).
Axes of the slice: x: 2, y: 2, z: 4, core: 2. Of those that a mesh axis runs over, the one named last changes fastest.
Arguments:
- latent_state: bfloat16 [32, 1024, 1024], P(('grp', 'fsdp')), may hold values from -6 to 6
- prelude_embed: bfloat16 [32, 1024, 1024], P(('grp', 'fsdp')), may hold values from -6 to 6
- out_grad: bfloat16 [32, 1024, 1024], P(('grp', 'fsdp')), may hold values from -6 to 6
- piece_starts: int32 [32, 2], P(('grp', 'fsdp')), may hold values from 0 to 768, as said below
- w_adapter: bfloat16 [2048, 1024], P('fsdp'), may hold values from -0.125 to 0.125
- w_query: bfloat16 [1024, 1024], P('fsdp'), may hold values from -0.1875 to 0.1875
- w_key: bfloat16 [1024, 1024], P('fsdp'), may hold values from -0.1875 to 0.1875
- w_value: bfloat16 [1024, 1024], P('fsdp'), may hold values from -0.1875 to 0.1875
- w_out: bfloat16 [1024, 1024], P('fsdp'), may hold values from -0.1875 to 0.1875
- w_gate: bfloat16 [1024, 2816], P('fsdp'), may hold values from -0.1875 to 0.1875
- w_up: bfloat16 [1024, 2816], P('fsdp'), may hold values from -0.1875 to 0.1875
- w_down: bfloat16 [2816, 1024], P('fsdp'), may hold values from -0.109375 to 0.109375
- gain_attn_in: bfloat16 [1024], P('fsdp'), may hold values from 0.099609375 to 1.8984375
- gain_attn_out: bfloat16 [1024], P('fsdp'), may hold values from 0.099609375 to 1.8984375
- gain_ffn_in: bfloat16 [1024], P('fsdp'), may hold values from 0.099609375 to 1.8984375
- gain_ffn_out: bfloat16 [1024], P('fsdp'), may hold values from 0.099609375 to 1.8984375
Outputs:
- block_output: bfloat16 [32, 1024, 1024], P(('grp', 'fsdp'))
- state_grad: bfloat16 [32, 1024, 1024], P(('grp', 'fsdp'))
- embed_grad: bfloat16 [32, 1024, 1024], P(('grp', 'fsdp'))
- adapter_grad: float32 [2048, 1024], P('fsdp')
- query_weight_grad: float32 [1024, 1024], P('fsdp')
- key_weight_grad: float32 [1024, 1024], P('fsdp')
- value_weight_grad: float32 [1024, 1024], P('fsdp')
- out_weight_grad: float32 [1024, 1024], P('fsdp')
- gate_weight_grad: float32 [1024, 2816], P('fsdp')
- up_weight_grad: float32 [1024, 2816], P('fsdp')
- down_weight_grad: float32 [2816, 1024], P('fsdp')
- gain_attn_in_grad: float32 [1024], P('fsdp')
- gain_attn_out_grad: float32 [1024], P('fsdp')
- gain_ffn_in_grad: float32 [1024], P('fsdp')
- gain_ffn_out_grad: float32 [1024], P('fsdp')
The draws below stay inside these ranges and needn't reach their ends.
Inputs may be any that keep to these rules, and one draw needn't show every extreme that they name: `piece_starts`: each sequence's 2 starts are increasing; piece k starts within positions k * (512) to (k + 1) * 512 - 256, so that it ends inside that slot.
All inputs are finite; a program needn't handle non-finite values.
Results may differ from the reference program's by a relative error of at most 0.02.
Values may be sent and summed in bfloat16 or wider, within the bound.
No kernel may reach another device: no remote copies, remote signals or barrier semaphores. Data moves between devices by JAX's collectives and lax.ppermute only.
A program may use at most 384 MiB of HBM per device.

```python
import jax
import jax.numpy as jnp
from jax import lax

D = 1024
HEADS = 16
HEAD_DIM = 64
FF = 2816
LENGTH = 1024
PIECE = 256
PIECES = 2
SEQS = 32


def draw_piece_starts(key, part):
    slot_len = LENGTH // PIECES
    offsets = jax.random.randint(key, (SEQS, PIECES), 0, slot_len - PIECE + 1, dtype=jnp.int32)
    offsets = offsets.at[0, 0].set(0).at[0, PIECES - 1].set(slot_len - PIECE)
    slot_base = jnp.arange(PIECES, dtype=jnp.int32) * slot_len
    return (offsets + slot_base[None, :]).astype(jnp.int32)


def steps_of(stream_key, dims, cuts, least, largest):
    factor_of = 1.0
    for dim, shards_of in cuts:
        heights = jax.random.uniform(jax.random.fold_in(jax.random.fold_in(stream_key, 6), dim), (shards_of,), jnp.float32, least / len(cuts), largest / len(cuts))
        factor_of = factor_of * jnp.repeat(jnp.exp(heights), dims[dim] // shards_of).reshape((-1,) + (1,) * (len(dims) - 1 - dim))
    return factor_of


def gaussian(key, extent, scale, limit, cuts=(), kind=jnp.bfloat16):
    factor_of = steps_of(key, extent, cuts, -0.22, 0.18) if cuts else 1.0
    drawn = jax.random.normal(key, extent, jnp.float32) * scale * factor_of
    return jnp.minimum(jnp.maximum(drawn, -limit), limit).astype(kind)


def setup_inputs(seed: int = 0) -> dict:
    splits = jax.random.split(jax.random.key(seed), 17)
    return {
        "latent_state": gaussian(splits[0], (SEQS, LENGTH, D), 1.0, 6.0, ((0, 32),)),
        "prelude_embed": gaussian(splits[1], (SEQS, LENGTH, D), 1.0, 6.0, ((0, 32),)),
        "out_grad": gaussian(splits[2], (SEQS, LENGTH, D), 1.0, 6.0, ((0, 32),)),
        "piece_starts": draw_piece_starts(jax.random.fold_in(splits[16], 71), 0),
        "w_adapter": gaussian(splits[4], (2 * D, D), (2 * D) ** -0.5, 0.125, ((0, 8),)),
        "w_query": gaussian(splits[5], (D, D), D ** -0.5, 0.1875, ((0, 8),)),
        "w_key": gaussian(splits[6], (D, D), D ** -0.5, 0.1875, ((0, 8),)),
        "w_value": gaussian(splits[7], (D, D), D ** -0.5, 0.1875, ((0, 8),)),
        "w_out": gaussian(splits[8], (D, D), D ** -0.5, 0.1875, ((0, 8),)),
        "w_gate": gaussian(splits[9], (D, FF), D ** -0.5, 0.1875, ((0, 8),)),
        "w_up": gaussian(splits[10], (D, FF), D ** -0.5, 0.1875, ((0, 8),)),
        "w_down": gaussian(splits[11], (FF, D), FF ** -0.5, 0.109375, ((0, 8),)),
        "gain_attn_in": jnp.clip(1.0 + 0.18 * jax.random.normal(splits[12], (D,), jnp.float32), 0.099609375, 1.8984375).astype(jnp.bfloat16),
        "gain_attn_out": jnp.clip(1.0 + 0.18 * jax.random.normal(splits[13], (D,), jnp.float32), 0.099609375, 1.8984375).astype(jnp.bfloat16),
        "gain_ffn_in": jnp.clip(1.0 + 0.18 * jax.random.normal(splits[14], (D,), jnp.float32), 0.099609375, 1.8984375).astype(jnp.bfloat16),
        "gain_ffn_out": jnp.clip(1.0 + 0.18 * jax.random.normal(splits[15], (D,), jnp.float32), 0.099609375, 1.8984375).astype(jnp.bfloat16),
    }


EPS = 1e-06
NEG = -1e+30
THETA = 50000.0

@jax.custom_vjp
def low(v):
    return lax.optimization_barrier(v.astype(jnp.bfloat16)).astype(jnp.float32)

@jax.custom_vjp
def low_back(v):
    return v

def low_keep(v):
    return (low(v), None)

def low_pass(kept, grad):
    return (grad,)

def back_keep(v):
    return (v, None)

def back_low(kept, grad):
    return (low(grad),)
low.defvjp(low_keep, low_pass)
low_back.defvjp(back_keep, back_low)

def matmul_high(left, right):
    return jnp.dot(left, right, precision=lax.Precision.HIGHEST, preferred_element_type=jnp.float32)

def rms_scale(value, gain):
    inverse = lax.rsqrt(lax.optimization_barrier(jnp.mean(value * value, axis=-1, keepdims=True)) + EPS)
    return value * inverse * gain

def rotary_tables(length, half):
    position = jnp.arange(length, dtype=jnp.float32)
    frequency = THETA ** (-jnp.arange(half, dtype=jnp.float32) / half)
    angles = position[:, None] * frequency[None, :]
    return (jnp.cos(angles)[:, None, :], jnp.sin(angles)[:, None, :])

def rotate(values, cosine, sine_table):
    half = values.shape[-1] // 2
    first = values[..., :half]
    second = values[..., half:]
    return jnp.concatenate([first * cosine - second * sine_table, second * cosine + first * sine_table], axis=-1)

def allowed_mask(starts, length):
    position = jnp.arange(length, dtype=jnp.int32)
    inside = (position[:, None] >= starts[None, :]) & (position[:, None] < starts[None, :] + PIECE)
    numbers = jnp.arange(1, starts.shape[0] + 1, dtype=jnp.int32)
    labels = lax.optimization_barrier(jnp.sum(jnp.where(inside, numbers[None, :], 0), axis=1))
    causal = position[None, :] <= position[:, None]
    shared = (labels[:, None] == labels[None, :]) & (labels[:, None] > 0)
    return causal | shared

def core_layer(weights, state_rows, embed_rows, allowed, cosine, sine_table):
    w_adapter, w_query, w_key, w_value, w_out, w_gate, w_up, w_down, gain_attn_in, gain_attn_out, gain_ffn_in, gain_ffn_out = weights
    length = state_rows.shape[0]
    joined = jnp.concatenate([state_rows, embed_rows], axis=1)
    hidden = low_back(matmul_high(joined, w_adapter))
    normed = low(rms_scale(hidden, gain_attn_in))
    query = low_back(matmul_high(normed, w_query)).reshape(length, HEADS, HEAD_DIM)
    key_proj = low_back(matmul_high(normed, w_key)).reshape(length, HEADS, HEAD_DIM)
    value_low = low(low_back(matmul_high(normed, w_value))).reshape(length, HEADS, HEAD_DIM)
    query_rot = low(rotate(query, cosine, sine_table))
    key_rot = low(rotate(key_proj, cosine, sine_table))
    raw_scores = low_back(jnp.einsum('qhd,khd->hqk', query_rot, key_rot, precision=lax.Precision.HIGHEST))
    scores = jnp.where(allowed[None], raw_scores * HEAD_DIM ** (-0.5), NEG)
    row_max = lax.optimization_barrier(jnp.max(scores, axis=-1, keepdims=True))
    exponent = jnp.exp(scores - row_max)
    probs = exponent / lax.optimization_barrier(jnp.sum(exponent, axis=-1, keepdims=True))
    probs_low = low(probs)
    attended = jnp.einsum('hqk,khd->qhd', probs_low, value_low, precision=lax.Precision.HIGHEST)
    attended = low(low_back(attended.reshape(length, D)))
    branch = low_back(matmul_high(attended, w_out))
    mixed = hidden + rms_scale(branch, gain_attn_out)
    ffn_in = low(rms_scale(mixed, gain_ffn_in))
    gate = low_back(matmul_high(ffn_in, w_gate))
    up_value = low_back(matmul_high(ffn_in, w_up))
    product = low(gate * jax.nn.sigmoid(gate) * up_value)
    ffn_out = low_back(matmul_high(product, w_down))
    return mixed + rms_scale(ffn_out, gain_ffn_out)

def add_pair(first, second):
    return first + second

def reference(latent_state, prelude_embed, out_grad, piece_starts, w_adapter, w_query, w_key, w_value, w_out, w_gate, w_up, w_down, gain_attn_in, gain_attn_out, gain_ffn_in, gain_ffn_out):
    weights = tuple((item.astype(jnp.float32) for item in (w_adapter, w_query, w_key, w_value, w_out, w_gate, w_up, w_down, gain_attn_in, gain_attn_out, gain_ffn_in, gain_ffn_out)))
    cosine, sine_table = rotary_tables(LENGTH, HEAD_DIM // 2)

    def one_sequence(totals, pieces):
        state_rows, embed_rows, grad_rows, starts = pieces
        allowed = allowed_mask(starts, LENGTH)

        def forward(params, state_in, embed_in):
            return core_layer(params, state_in, embed_in, allowed, cosine, sine_table)
        output, pullback = jax.vjp(forward, weights, state_rows.astype(jnp.float32), embed_rows.astype(jnp.float32))
        weight_grads, state_part, embed_part = pullback(grad_rows.astype(jnp.float32))
        totals = jax.tree.map(add_pair, totals, weight_grads)
        return (totals, (output.astype(jnp.bfloat16), state_part.astype(jnp.bfloat16), embed_part.astype(jnp.bfloat16)))
    empty_sums = tuple((jnp.zeros_like(item) for item in weights))
    totals, stacked = lax.scan(one_sequence, empty_sums, (latent_state, prelude_embed, out_grad, piece_starts))
    return (stacked[0], stacked[1], stacked[2], totals[0], totals[1], totals[2], totals[3], totals[4], totals[5], totals[6], totals[7], totals[8], totals[9], totals[10], totals[11])
```

```python
import functools

import jax
import jax.numpy as jnp
from jax import lax
from jax.experimental import pallas as pl
from jax.experimental.pallas import tpu as pltpu
from jax.sharding import PartitionSpec as P

HEADS = 16
HEAD_DIM = 64
PIECE = 256
PAIR = 2 * HEAD_DIM
GAIN_ROWS = 8

EPS = 1e-06
NEG = -1e30
THETA = 50000.0
AXES = ("grp", "fsdp")
F32 = jnp.float32
BF = jnp.bfloat16


def rms_parts(value, gain):
    inverse = lax.rsqrt(jnp.mean(value * value, axis=-1, keepdims=True) + EPS)
    return (value * inverse * gain, inverse)


def norm_back(value, inverse, gain, grad_out):
    scaled = gain * grad_out
    gain_grad = jnp.sum(grad_out * value * inverse, axis=0)
    cubed = inverse * inverse * inverse
    value_grad = inverse * scaled - value * cubed * jnp.mean(scaled * value, axis=-1, keepdims=True)
    return (value_grad, gain_grad)


def dot(left, right, left_dim, right_dim):
    return lax.dot_general(
        left, right, (((left_dim,), (right_dim,)), ((), ())), preferred_element_type=F32
    )


def fill_bias(starts_ref, bias_ref, length):
    rows = 128

    def step(i, carry):
        key_pos = lax.broadcasted_iota(jnp.int32, (rows, length), 0) + i * rows
        query_pos = lax.broadcasted_iota(jnp.int32, (rows, length), 1)
        allowed = key_pos <= query_pos
        for k in range(2):
            first = starts_ref[0, k]
            last = first + PIECE
            allowed = allowed | (
                (key_pos >= first) & (key_pos < last) & (query_pos >= first) & (query_pos < last)
            )
        bias_ref[pl.ds(pl.multiple_of(i * rows, rows), rows), :] = jnp.where(allowed, 0.0, NEG)
        return carry

    lax.fori_loop(0, length // rows, step, 0)


def swap_halves(values):
    width = values.shape[1]
    half = HEAD_DIM // 2
    lane = lax.broadcasted_iota(jnp.int32, values.shape, 1)
    return jnp.where(
        (lane % HEAD_DIM) < half,
        pltpu.roll(values, width - half, 1),
        pltpu.roll(values, half, 1),
    )


def extents(length, rows):
    slot = length // 2
    return [(lo, ((lo + rows - 1) // slot + 1) * slot) for lo in range(0, length, rows)]


def add_bias(scores, bias_ref, lo, hi, rows):
    if lo == 0:
        return scores + bias_ref[lo:hi, lo : lo + rows]
    return jnp.concatenate(
        [scores[:lo], scores[lo:] + bias_ref[lo:hi, lo : lo + rows]], axis=0
    )


def forward_kernel(
    starts_ref, q_ref, k_ref, v_ref, cos_ref, sin_ref, o_ref, qr_ref, kr_ref, lse_ref, bias_ref,
    *, length, rows
):
    @pl.when(pl.program_id(0) == 0)
    def _():
        fill_bias(starts_ref, bias_ref, length)

    cosine = cos_ref[...]
    sine = sin_ref[...]
    query = q_ref[...]
    key = k_ref[...]
    query_rot = (query * cosine + swap_halves(query) * sine).astype(BF) * BF(HEAD_DIM**-0.5)
    key_rot = (key * cosine + swap_halves(key) * sine).astype(BF)
    qr_ref[...] = query_rot
    kr_ref[...] = key_rot
    value_t = v_ref[...].T
    low = lax.broadcasted_iota(jnp.int32, (length, PAIR), 1) < HEAD_DIM
    zero = BF(0)
    keys = (jnp.where(low, key_rot, zero), jnp.where(low, zero, key_rot))
    for lo, hi in extents(length, rows):
        block = query_rot[lo : lo + rows]
        outs = []
        for a in range(2):
            scores = add_bias(dot(keys[a][:hi], block, 1, 1), bias_ref, lo, hi, rows)
            top = jnp.max(scores, axis=0, keepdims=True)
            exponent = jnp.exp(scores - top)
            total = jnp.sum(exponent, axis=0, keepdims=True)
            lse_ref[0, a : a + 1, lo : lo + rows] = top + jnp.log(total)
            probs = (exponent * (1.0 / total)).astype(BF)
            outs.append(dot(value_t[HEAD_DIM * a : HEAD_DIM * (a + 1), :hi], probs, 1, 0))
        o_ref[lo : lo + rows, :] = jnp.concatenate(outs, 0).T.astype(BF)


def backward_kernel(
    starts_ref, q_ref, k_ref, v_ref, g_ref, o_ref, lse_ref, cos_ref, sin_ref,
    dq_ref, dk_ref, dv_ref, bias_ref, *, length, rows
):
    @pl.when(pl.program_id(0) == 0)
    def _():
        fill_bias(starts_ref, bias_ref, length)

    query_rot = q_ref[...]
    key_rot = k_ref[...]
    value = v_ref[...]
    grad = g_ref[...]
    low = lax.broadcasted_iota(jnp.int32, (length, PAIR), 1) < HEAD_DIM
    zero = BF(0)

    def only(array, a):
        mask = low[: array.shape[0]]
        return jnp.where(mask, array, zero) if a == 0 else jnp.where(mask, zero, array)

    keys = (only(key_rot, 0), only(key_rot, 1))
    values = (only(value, 0), only(value, 1))
    key_t = key_rot.T
    product = grad.astype(F32) * o_ref[...].astype(F32)
    key_grad = jnp.zeros((length, PAIR), F32)
    value_grad = jnp.zeros((length, PAIR), F32)
    cosine = cos_ref[...]
    sine = sin_ref[...]

    def turn_back(array, lo, count):
        return array * cosine[lo : lo + count] - swap_halves(array) * sine[lo : lo + count]

    def add_rows(total, part, hi):
        if hi == length:
            return total + part
        return jnp.concatenate([total[:hi] + part, total[hi:]], axis=0)

    for lo, hi in extents(length, rows):
        query_block = query_rot[lo : lo + rows]
        grad_block = grad[lo : lo + rows]
        product_t = product[lo : lo + rows].T
        parts = []
        for a in range(2):
            delta = jnp.sum(product_t[HEAD_DIM * a : HEAD_DIM * (a + 1)], axis=0, keepdims=True)
            scores = dot(keys[a][:hi], query_block, 1, 1) - lse_ref[0, a : a + 1, lo : lo + rows]
            probs = jnp.exp(add_bias(scores, bias_ref, lo, hi, rows))
            probs_grad = dot(values[a][:hi], grad_block, 1, 1)
            score_grad = (probs * (probs_grad - delta)).astype(BF)
            value_grad = add_rows(value_grad, dot(probs.astype(BF), only(grad_block, a), 1, 0), hi)
            key_grad = add_rows(key_grad, dot(score_grad, only(query_block, a), 1, 0), hi)
            parts.append(dot(key_t[HEAD_DIM * a : HEAD_DIM * (a + 1), :hi], score_grad, 1, 0))
        query_grad = (jnp.concatenate(parts, 0) * HEAD_DIM**-0.5).T
        dq_ref[lo : lo + rows, :] = turn_back(query_grad, lo, rows).astype(BF)
    dk_ref[...] = turn_back(key_grad, 0, length).astype(BF)
    dv_ref[...] = value_grad.astype(BF)


def rotary_tables(length):
    half = HEAD_DIM // 2
    position = jnp.arange(length, dtype=F32)
    frequency = THETA ** (-jnp.arange(half, dtype=F32) / half)
    angles = position[:, None] * frequency[None, :]
    cosine, sine = jnp.cos(angles), jnp.sin(angles)
    return (
        jnp.concatenate([cosine] * 4, axis=1),
        jnp.concatenate([-sine, sine, -sine, sine], axis=1),
    )


def attention_specs(length):
    column = pl.BlockSpec((length, PAIR), lambda i: (0, i))
    table = pl.BlockSpec((length, PAIR), lambda i: (0, 0))
    sums = pl.BlockSpec((1, 2, length), lambda i: (i, 0, 0))
    return pl.BlockSpec(memory_space=pltpu.SMEM), column, table, sums


def attention_forward(starts, query, key, value, cosine, sine, rows=256):
    length, width = query.shape
    count = width // PAIR
    scalars, column, table, sums = attention_specs(length)
    half = jax.ShapeDtypeStruct((length, width), BF)
    return pl.pallas_call(
        functools.partial(forward_kernel, length=length, rows=rows),
        grid=(count,),
        in_specs=[scalars, column, column, column, table, table],
        out_specs=[column, column, column, sums],
        out_shape=[half, half, half, jax.ShapeDtypeStruct((count, 2, length), F32)],
        scratch_shapes=[pltpu.VMEM((length, length), F32)],
        compiler_params=pltpu.CompilerParams(vmem_limit_bytes=48 << 20),
        cost_estimate=pl.CostEstimate(
            flops=25_000_000_000, transcendentals=length * length * 12, bytes_accessed=20 << 20
        ),
        name="attention_forward",
    )(starts, query, key, value, cosine, sine)


def attention_backward(starts, query_rot, key_rot, value, grad, attended, lse, cosine, sine, rows=256):
    length, width = query_rot.shape
    count = width // PAIR
    scalars, column, table, sums = attention_specs(length)
    half = jax.ShapeDtypeStruct((length, width), BF)
    return pl.pallas_call(
        functools.partial(backward_kernel, length=length, rows=rows),
        grid=(count,),
        in_specs=[scalars, column, column, column, column, column, sums, table, table],
        out_specs=[column, column, column],
        out_shape=[half, half, half],
        scratch_shapes=[pltpu.VMEM((length, length), F32)],
        compiler_params=pltpu.CompilerParams(vmem_limit_bytes=48 << 20),
        cost_estimate=pl.CostEstimate(
            flops=25_000_000_000, transcendentals=length * length * 12, bytes_accessed=20 << 20
        ),
        name="attention_backward",
    )(starts, query_rot, key_rot, value, grad, attended, lse, cosine, sine)


class Links:
    X, CORE, Z1, Z3, Y = 16, 8, 2, 6, 1

    def __init__(self):
        group = lax.axis_index("grp")
        shard = lax.axis_index("fsdp")
        self.x, self.core = group // 2, group % 2
        self.z, self.y = shard // 2, shard % 2

    def swap(self, value, bits):
        return lax.ppermute(value, AXES, [(d, d ^ bits) for d in range(32)])


def take(value, start, size, axis):
    return lax.dynamic_slice_in_dim(value, start, size, axis)


def join_kernel(place_ref, *refs, quarters):
    zs, zc, ry, yc, rx, xc = refs[:6]
    outs = refs[6 : 6 + len(quarters)]
    sems = refs[6 + len(quarters)]
    z, y, core, x = (place_ref[i] for i in range(4))
    copies = []

    def copy(source, target):
        copies.append(pltpu.make_async_copy(source, target, sems.at[len(copies)]))
        copies[-1].start()

    offset = 0
    for out, count in zip(outs, quarters):
        part = pl.ds(offset, count)
        offset += count
        for r in range(4):
            row = (z ^ r) * 2
            copy(zs.at[r, :, part], out.at[row + y, pl.ds(2 * core, 2)])
            copy(zc.at[r, :, part], out.at[row + y, pl.ds(2 - 2 * core, 2)])
            copy(ry.at[r, part], out.at[row + 1 - y, 2 * core + x])
            copy(rx.at[r, part], out.at[row + 1 - y, 2 * core + 1 - x])
            copy(yc.at[r, part], out.at[row + 1 - y, 2 - 2 * core + x])
            copy(xc.at[r, part], out.at[row + 1 - y, 3 - 2 * core - x])
    for item in copies:
        item.wait()


def gather_linked(links, pieces):
    columns = pieces[0].shape[1]
    quarters = [piece.shape[0] // 4 for piece in pieces]
    packed = [piece.reshape(4, -1, columns) for piece in pieces]
    packed = packed[0] if len(packed) == 1 else jnp.concatenate(packed, axis=1)
    mine = take(packed, 2 * links.core, 2, 0)
    near = links.swap(mine, links.Z1)
    far = links.swap(mine, links.Z3)
    second = links.swap(far, links.Z1)
    zs = jnp.stack([mine, near, second, far])
    ry = links.swap(take(zs, links.x, 1, 1)[:, 0], links.Y)
    rx = links.swap(ry, links.X)
    zc, yc, xc = (links.swap(item, links.CORE) for item in (zs, ry, rx))
    place = jnp.stack([links.z, links.y, links.core, links.x]).astype(jnp.int32)
    anywhere = pl.BlockSpec(memory_space=pl.ANY)
    outs = pl.pallas_call(
        functools.partial(join_kernel, quarters=quarters),
        in_specs=[pl.BlockSpec(memory_space=pltpu.SMEM)] + [anywhere] * 6,
        out_specs=[anywhere] * len(quarters),
        out_shape=[jax.ShapeDtypeStruct((8, 4, q, columns), BF) for q in quarters],
        scratch_shapes=[pltpu.SemaphoreType.DMA((24 * len(quarters),))],
        name="join",
    )(place, zs, zc, ry, yc, rx, xc)
    return [out.reshape(32 * q, columns) for out, q in zip(outs, quarters)]


def scatter_linked(links, grads):
    columns = grads[0].shape[1]
    quarters = [grad.shape[0] // 32 for grad in grads]
    whole = [grad.reshape(8, 4, q, columns) for grad, q in zip(grads, quarters)]

    def half(which):
        parts = [take(item, 2 * which, 2, 1) for item in whole]
        return parts[0] if len(parts) == 1 else jnp.concatenate(parts, axis=2)

    both = half(links.core) + links.swap(half(1 - links.core), links.CORE)
    both = both.reshape(4, 2, 2, sum(quarters), columns)
    other = take(both, 1 - links.y, 1, 1)[:, 0]
    other = take(other, links.x, 1, 1) + links.swap(take(other, 1 - links.x, 1, 1), links.X)
    other = links.swap(other, links.Y)
    own = take(both, links.y, 1, 1)[:, 0]
    own = lax.dynamic_update_slice_in_dim(own, take(own, links.x, 1, 1) + other, links.x, 1)

    def at(bits):
        return take(own, links.z ^ bits, 1, 0)[0]

    second = links.swap(at(2), links.Z1)
    near = links.swap(at(1), links.Z1)
    far = links.swap(at(3) + second, links.Z3)
    total = at(0) + near + far
    total = total + links.swap(total, links.X)
    twin = links.swap(total, links.CORE)
    total = jnp.where(
        links.core == 0,
        jnp.concatenate([total, twin], axis=0),
        jnp.concatenate([twin, total], axis=0),
    ).astype(F32)
    results = []
    offset = 0
    for q in quarters:
        results.append(total[:, offset : offset + q].reshape(4 * q, columns))
        offset += q
    return results


class Plain:
    pass


def gather(links, pieces):
    if links is not None:
        return gather_linked(links, pieces)
    return [lax.all_gather(piece, "fsdp", axis=0, tiled=True) for piece in pieces]


def scatter(links, grads):
    if links is not None:
        return scatter_linked(links, grads)
    return [
        lax.psum(lax.psum_scatter(grad, "fsdp", scatter_dimension=0, tiled=True), "grp").astype(F32)
        for grad in grads
    ]


def pack_gains(gains):
    rows = jnp.stack(gains)
    width = 1024
    return jnp.pad(rows[:, None], ((0, 0), (0, GAIN_ROWS - 1), (0, width - rows.shape[1]))).reshape(
        4 * GAIN_ROWS, width
    )


def unpack_gains(rows, shards, size):
    rows = rows.reshape(shards, 4, GAIN_ROWS, -1)[:, :, 0, :size]
    return [rows[:, j].reshape(shards * size).astype(F32) for j in range(4)]


def pack_gain_grads(grads, shards):
    rows = jnp.stack([grad.reshape(shards, -1) for grad in grads], axis=1).astype(BF)
    return jnp.pad(
        rows[:, :, None], ((0, 0), (0, 0), (0, GAIN_ROWS - 1), (0, 1024 - rows.shape[2]))
    ).reshape(shards * 4 * GAIN_ROWS, 1024)


def matmul(left, right, left_dim, right_dim, kind=F32):
    return dot(left, right, left_dim, right_dim).astype(kind)


def body(
    latent_state,
    prelude_embed,
    out_grad,
    piece_starts,
    w_adapter,
    w_query,
    w_key,
    w_value,
    w_out,
    w_gate,
    w_up,
    w_down,
    gain_attn_in,
    gain_attn_out,
    gain_ffn_in,
    gain_ffn_out,
    *,
    shards,
    linked,
):
    links = Links() if linked else None
    gains = pack_gains([gain_attn_in, gain_attn_out, gain_ffn_in, gain_ffn_out])
    (adapter,) = gather(links, [w_adapter])
    wq, wk, wv, wo, gains = gather(links, [w_query, w_key, w_value, w_out, gains])
    gate_w, up_w = gather(links, [w_gate, w_up])
    (down_w,) = gather(links, [w_down])
    gain_one, gain_two, gain_three, gain_four = unpack_gains(gains, shards, gain_attn_in.shape[0])

    seq_count, length, width = latent_state.shape
    joined = jnp.concatenate([latent_state, prelude_embed], axis=2).reshape(length, 2 * width)
    hidden = matmul(joined, adapter, 1, 0)
    normed, inverse_one = rms_parts(hidden, gain_one)
    normed = normed.astype(BF)
    cosine, sine = rotary_tables(length)
    query = matmul(normed, wq, 1, 0)
    key = matmul(normed, wk, 1, 0)
    value = matmul(normed, wv, 1, 0, BF)
    attended, query_rot, key_rot, lse = attention_forward(
        piece_starts, query, key, value, cosine, sine
    )
    branch = matmul(attended, wo, 1, 0)
    branch_normed, inverse_two = rms_parts(branch, gain_two)
    mixed = hidden + branch_normed
    ffn_in, inverse_three = rms_parts(mixed, gain_three)
    ffn_in = ffn_in.astype(BF)
    gate = matmul(ffn_in, gate_w, 1, 0)
    up_value = matmul(ffn_in, up_w, 1, 0)
    sigmoid_gate = jax.nn.sigmoid(gate)
    product = (gate * sigmoid_gate * up_value).astype(BF)
    ffn_out = matmul(product, down_w, 1, 0)
    ffn_normed, inverse_four = rms_parts(ffn_out, gain_four)
    block_output = (mixed + ffn_normed).astype(BF).reshape(seq_count, length, width)

    grad_rows = out_grad.reshape(length, width).astype(F32)
    ffn_grad, gain_four_grad = norm_back(ffn_out, inverse_four, gain_four, grad_rows)
    ffn_grad = ffn_grad.astype(BF)
    down_grad = matmul(product, ffn_grad, 0, 0, BF)
    (down_grad,) = scatter(links, [down_grad])
    product_grad = matmul(ffn_grad, down_w, 1, 1)
    gate_grad = (
        product_grad * up_value * (sigmoid_gate * (1.0 + gate * (1.0 - sigmoid_gate)))
    ).astype(BF)
    up_grad = (product_grad * (gate * sigmoid_gate)).astype(BF)
    gate_weight_grad = matmul(ffn_in, gate_grad, 0, 0, BF)
    up_weight_grad = matmul(ffn_in, up_grad, 0, 0, BF)
    gate_weight_grad, up_weight_grad = scatter(links, [gate_weight_grad, up_weight_grad])
    ffn_in_grad = matmul(gate_grad, gate_w, 1, 1) + matmul(up_grad, up_w, 1, 1)
    mixed_part, gain_three_grad = norm_back(mixed, inverse_three, gain_three, ffn_in_grad)
    mixed_grad = grad_rows + mixed_part
    branch_grad, gain_two_grad = norm_back(branch, inverse_two, gain_two, mixed_grad)
    branch_grad = branch_grad.astype(BF)
    out_weight_grad = matmul(attended, branch_grad, 0, 0, BF)
    attended_grad = matmul(branch_grad, wo, 1, 1, BF)
    query_grad, key_grad, value_grad = attention_backward(
        piece_starts, query_rot, key_rot, value, attended_grad, attended, lse, cosine, sine
    )
    query_weight_grad = matmul(normed, query_grad, 0, 0, BF)
    key_weight_grad = matmul(normed, key_grad, 0, 0, BF)
    value_weight_grad = matmul(normed, value_grad, 0, 0, BF)
    out_weight_grad, query_weight_grad, key_weight_grad, value_weight_grad = scatter(
        links, [out_weight_grad, query_weight_grad, key_weight_grad, value_weight_grad]
    )
    normed_grad = (
        matmul(query_grad, wq, 1, 1) + matmul(key_grad, wk, 1, 1) + matmul(value_grad, wv, 1, 1)
    )
    hidden_part, gain_one_grad = norm_back(hidden, inverse_one, gain_one, normed_grad)
    hidden_grad = (mixed_grad + hidden_part).astype(BF)
    adapter_grad = matmul(joined, hidden_grad, 0, 0, BF)
    gain_grads = pack_gain_grads(
        [gain_one_grad, gain_two_grad, gain_three_grad, gain_four_grad], shards
    )
    adapter_grad, gain_grads = scatter(links, [adapter_grad, gain_grads])
    gain_grads = unpack_gains(gain_grads, 1, gain_attn_in.shape[0])
    joined_grad = matmul(hidden_grad, adapter, 1, 1, BF).reshape(seq_count, length, 2 * width)
    return (
        block_output,
        joined_grad[..., :width],
        joined_grad[..., width:],
        adapter_grad,
        query_weight_grad,
        key_weight_grad,
        value_weight_grad,
        out_weight_grad,
        gate_weight_grad,
        up_weight_grad,
        down_grad,
        *gain_grads,
    )


def solution(mesh):
    rows = P(("grp", "fsdp"), None, None)
    matrix = P("fsdp", None)
    vector = P("fsdp")
    in_specs = (rows,) * 3 + (P(("grp", "fsdp"), None),) + (matrix,) * 8 + (vector,) * 4
    out_specs = (rows,) * 3 + (matrix,) * 8 + (vector,) * 4
    shards = mesh.shape["fsdp"]
    linked = (mesh.shape["grp"], shards) == (4, 8)
    return jax.shard_map(
        functools.partial(body, shards=shards, linked=linked),
        mesh=mesh,
        in_specs=in_specs,
        out_specs=out_specs,
        check_vma=False,
    )
```

```python
import functools

import jax
import jax.numpy as jnp
from jax import lax
from jax.experimental import pallas as pl
from jax.experimental.pallas import tpu as pltpu
from jax.sharding import PartitionSpec as P

HEADS = 16
HEAD_DIM = 64
PIECE = 256
PAIR = 2 * HEAD_DIM
GAIN_ROWS = 8

EPS = 1e-06
NEG = -1e30
THETA = 50000.0
AXES = ("grp", "fsdp")
F32 = jnp.float32
BF = jnp.bfloat16


def rms_parts(value, gain):
    inverse = lax.rsqrt(jnp.mean(value * value, axis=-1, keepdims=True) + EPS)
    return (value * inverse * gain, inverse)


def norm_back(value, inverse, gain, grad_out):
    scaled = gain * grad_out
    gain_grad = jnp.sum(grad_out * value * inverse, axis=0)
    cubed = inverse * inverse * inverse
    value_grad = inverse * scaled - value * cubed * jnp.mean(scaled * value, axis=-1, keepdims=True)
    return (value_grad, gain_grad)


def dot(left, right, left_dim, right_dim):
    return lax.dot_general(
        left, right, (((left_dim,), (right_dim,)), ((), ())), preferred_element_type=F32
    )


def fill_bias(starts_ref, bias_ref, length):
    rows = 128

    def step(i, carry):
        key_pos = lax.broadcasted_iota(jnp.int32, (rows, length), 0) + i * rows
        query_pos = lax.broadcasted_iota(jnp.int32, (rows, length), 1)
        allowed = key_pos <= query_pos
        for k in range(2):
            first = starts_ref[0, k]
            last = first + PIECE
            allowed = allowed | (
                (key_pos >= first) & (key_pos < last) & (query_pos >= first) & (query_pos < last)
            )
        bias_ref[pl.ds(pl.multiple_of(i * rows, rows), rows), :] = jnp.where(allowed, 0.0, NEG)
        return carry

    lax.fori_loop(0, length // rows, step, 0)


def swap_halves(values):
    width = values.shape[1]
    half = HEAD_DIM // 2
    lane = lax.broadcasted_iota(jnp.int32, values.shape, 1)
    return jnp.where(
        (lane % HEAD_DIM) < half,
        pltpu.roll(values, width - half, 1),
        pltpu.roll(values, half, 1),
    )


def extents(length, rows):
    slot = length // 2
    return [(lo, ((lo + rows - 1) // slot + 1) * slot) for lo in range(0, length, rows)]


def add_bias(scores, bias_ref, lo, hi, rows):
    if lo == 0:
        return scores + bias_ref[lo:hi, lo : lo + rows]
    return jnp.concatenate(
        [scores[:lo], scores[lo:] + bias_ref[lo:hi, lo : lo + rows]], axis=0
    )


def forward_kernel(
    starts_ref, q_ref, k_ref, v_ref, cos_ref, sin_ref, o_ref, qr_ref, kr_ref, lse_ref, bias_ref,
    *, length, rows
):
    @pl.when(pl.program_id(0) == 0)
    def _():
        fill_bias(starts_ref, bias_ref, length)

    cosine = cos_ref[...]
    sine = sin_ref[...]
    query = q_ref[...]
    key = k_ref[...]
    query_rot = (query * cosine + swap_halves(query) * sine).astype(BF) * BF(HEAD_DIM**-0.5)
    key_rot = (key * cosine + swap_halves(key) * sine).astype(BF)
    qr_ref[...] = query_rot
    kr_ref[...] = key_rot
    value_t = v_ref[...].T
    low = lax.broadcasted_iota(jnp.int32, (length, PAIR), 1) < HEAD_DIM
    zero = BF(0)
    keys = (jnp.where(low, key_rot, zero), jnp.where(low, zero, key_rot))
    for lo, hi in extents(length, rows):
        block = query_rot[lo : lo + rows]
        outs = []
        for a in range(2):
            scores = add_bias(dot(keys[a][:hi], block, 1, 1), bias_ref, lo, hi, rows)
            top = jnp.max(scores, axis=0, keepdims=True)
            exponent = jnp.exp(scores - top)
            total = jnp.sum(exponent, axis=0, keepdims=True)
            lse_ref[0, a : a + 1, lo : lo + rows] = top + jnp.log(total)
            probs = (exponent * (1.0 / total)).astype(BF)
            outs.append(dot(value_t[HEAD_DIM * a : HEAD_DIM * (a + 1), :hi], probs, 1, 0))
        o_ref[lo : lo + rows, :] = jnp.concatenate(outs, 0).T.astype(BF)


def backward_kernel(
    starts_ref, q_ref, k_ref, v_ref, g_ref, o_ref, lse_ref, cos_ref, sin_ref,
    dq_ref, dk_ref, dv_ref, bias_ref, *, length, rows
):
    @pl.when(pl.program_id(0) == 0)
    def _():
        fill_bias(starts_ref, bias_ref, length)

    query_rot = q_ref[...]
    key_rot = k_ref[...]
    value = v_ref[...]
    grad = g_ref[...]
    low = lax.broadcasted_iota(jnp.int32, (length, PAIR), 1) < HEAD_DIM
    zero = BF(0)

    def only(array, a):
        mask = low[: array.shape[0]]
        return jnp.where(mask, array, zero) if a == 0 else jnp.where(mask, zero, array)

    keys = (only(key_rot, 0), only(key_rot, 1))
    values = (only(value, 0), only(value, 1))
    key_t = key_rot.T
    product = grad.astype(F32) * o_ref[...].astype(F32)
    key_grad = jnp.zeros((length, PAIR), F32)
    value_grad = jnp.zeros((length, PAIR), F32)
    cosine = cos_ref[...]
    sine = sin_ref[...]

    def turn_back(array, lo, count):
        return array * cosine[lo : lo + count] - swap_halves(array) * sine[lo : lo + count]

    def add_rows(total, part, hi):
        if hi == length:
            return total + part
        return jnp.concatenate([total[:hi] + part, total[hi:]], axis=0)

    for lo, hi in extents(length, rows):
        query_block = query_rot[lo : lo + rows]
        grad_block = grad[lo : lo + rows]
        product_t = product[lo : lo + rows].T
        parts = []
        for a in range(2):
            delta = jnp.sum(product_t[HEAD_DIM * a : HEAD_DIM * (a + 1)], axis=0, keepdims=True)
            scores = dot(keys[a][:hi], query_block, 1, 1) - lse_ref[0, a : a + 1, lo : lo + rows]
            probs = jnp.exp(add_bias(scores, bias_ref, lo, hi, rows))
            probs_grad = dot(values[a][:hi], grad_block, 1, 1)
            score_grad = (probs * (probs_grad - delta)).astype(BF)
            value_grad = add_rows(value_grad, dot(probs.astype(BF), only(grad_block, a), 1, 0), hi)
            key_grad = add_rows(key_grad, dot(score_grad, only(query_block, a), 1, 0), hi)
            parts.append(dot(key_t[HEAD_DIM * a : HEAD_DIM * (a + 1), :hi], score_grad, 1, 0))
        query_grad = (jnp.concatenate(parts, 0) * HEAD_DIM**-0.5).T
        dq_ref[lo : lo + rows, :] = turn_back(query_grad, lo, rows).astype(BF)
    dk_ref[...] = turn_back(key_grad, 0, length).astype(BF)
    dv_ref[...] = value_grad.astype(BF)


def rotary_tables(length):
    half = HEAD_DIM // 2
    position = jnp.arange(length, dtype=F32)
    frequency = THETA ** (-jnp.arange(half, dtype=F32) / half)
    angles = position[:, None] * frequency[None, :]
    cosine, sine = jnp.cos(angles), jnp.sin(angles)
    return (
        jnp.concatenate([cosine] * 4, axis=1),
        jnp.concatenate([-sine, sine, -sine, sine], axis=1),
    )


def attention_specs(length, first):
    column = pl.BlockSpec((length, PAIR), lambda i: (0, i + first))
    table = pl.BlockSpec((length, PAIR), lambda i: (0, 0))
    sums = pl.BlockSpec((1, 2, length), lambda i: (i + first, 0, 0))
    return pl.BlockSpec(memory_space=pltpu.SMEM), column, table, sums


def without_refs(kernel, place, count):
    def run(*refs):
        return kernel(*refs[:place], *refs[place + count :])

    return run


def attention_call(kernel, name, length, width, steps, first, inputs, in_specs, out_specs, out_shape, earlier):
    anywhere = pl.BlockSpec(memory_space=pl.ANY)
    count = len(inputs)
    earlier = list(earlier or ())
    return pl.pallas_call(
        without_refs(kernel, count, len(earlier)),
        grid=(steps,),
        in_specs=in_specs + [anywhere] * len(earlier),
        out_specs=out_specs,
        out_shape=out_shape,
        scratch_shapes=[pltpu.VMEM((length, length), F32)],
        input_output_aliases={count + i: i for i in range(len(earlier))},
        compiler_params=pltpu.CompilerParams(vmem_limit_bytes=48 << 20),
        cost_estimate=pl.CostEstimate(
            flops=steps * 2_000_000_000,
            transcendentals=length * length * steps * 2,
            bytes_accessed=steps << 21,
        ),
        name=name,
    )(*inputs, *earlier)


def attention_forward(starts, query, key, value, cosine, sine, steps, first, earlier, rows=256):
    length, width = query.shape
    count = width // PAIR
    scalars, column, table, sums = attention_specs(length, first)
    half = jax.ShapeDtypeStruct((length, width), BF)
    return attention_call(
        functools.partial(forward_kernel, length=length, rows=rows),
        "attention_forward",
        length,
        width,
        steps,
        first,
        [starts, query, key, value, cosine, sine],
        [scalars, column, column, column, table, table],
        [column, column, column, sums],
        [half, half, half, jax.ShapeDtypeStruct((count, 2, length), F32)],
        earlier,
    )


def attention_backward(
    starts, query_rot, key_rot, value, grad, attended, lse, cosine, sine, steps, first, earlier, rows=256
):
    length, width = query_rot.shape
    scalars, column, table, sums = attention_specs(length, first)
    half = jax.ShapeDtypeStruct((length, width), BF)
    return attention_call(
        functools.partial(backward_kernel, length=length, rows=rows),
        "attention_backward",
        length,
        width,
        steps,
        first,
        [starts, query_rot, key_rot, value, grad, attended, lse, cosine, sine],
        [scalars, column, column, column, column, column, sums, table, table],
        [column, column, column],
        [half, half, half],
        earlier,
    )


class Links:
    X, CORE, Z1, Z3, Y = 16, 8, 2, 6, 1

    def __init__(self):
        group = lax.axis_index("grp")
        shard = lax.axis_index("fsdp")
        self.x, self.core = group // 2, group % 2
        self.z, self.y = shard // 2, shard % 2

    def swap(self, value, bits):
        return lax.ppermute(value, AXES, [(d, d ^ bits) for d in range(32)])


def take(value, start, size, axis):
    return lax.dynamic_slice_in_dim(value, start, size, axis)


def join_kernel(place_ref, *refs, quarters, split):
    count = 6 if split else 4
    zs, zc, ry, yc = refs[:4]
    rx, xc = refs[4:6] if split else (None, None)
    outs = refs[count : count + len(quarters)]
    sems = refs[count + len(quarters)]
    z, y, core, x = (place_ref[i] for i in range(4))
    copies = []

    def copy(source, target):
        copies.append(pltpu.make_async_copy(source, target, sems.at[len(copies)]))
        copies[-1].start()

    offset = 0
    for out, size in zip(outs, quarters):
        part = pl.ds(offset, size)
        offset += size
        here, there = pl.ds(2 * core, 2), pl.ds(2 - 2 * core, 2)
        for r in range(4):
            row = (z ^ r) * 2
            copy(zs.at[r, :, part], out.at[row + y, here])
            copy(zc.at[r, :, part], out.at[row + y, there])
            if split:
                copy(ry.at[r, part], out.at[row + 1 - y, 2 * core + x])
                copy(rx.at[r, part], out.at[row + 1 - y, 2 * core + 1 - x])
                copy(yc.at[r, part], out.at[row + 1 - y, 2 - 2 * core + x])
                copy(xc.at[r, part], out.at[row + 1 - y, 3 - 2 * core - x])
            else:
                copy(ry.at[r, :, part], out.at[row + 1 - y, here])
                copy(yc.at[r, :, part], out.at[row + 1 - y, there])
    for item in copies:
        item.wait()


def gather_task(links, pieces, split):
    columns = pieces[0].shape[1]
    quarters = [piece.shape[0] // 4 for piece in pieces]
    packed = [piece.reshape(4, -1, columns) for piece in pieces]
    packed = packed[0] if len(packed) == 1 else jnp.concatenate(packed, axis=1)
    mine = take(packed, 2 * links.core, 2, 0)
    far = links.swap(mine, links.Z3)
    near = links.swap(mine, links.Z1)
    mine, near, far = yield (mine, near, far)
    second = links.swap(far, links.Z1)
    (second,) = yield (second,)
    zs = jnp.stack([mine, near, second, far])
    ry = links.swap(take(zs, links.x, 1, 1)[:, 0] if split else zs, links.Y)
    zs, ry = yield (zs, ry)
    parts = [zs, ry]
    if split:
        rx = links.swap(ry, links.X)
        (rx,) = yield (rx,)
        parts.append(rx)
    twins = [links.swap(item, links.CORE) for item in parts]
    twins = yield tuple(twins)
    refs = [item for pair in zip(parts, twins) for item in pair]
    place = jnp.stack([links.z, links.y, links.core, links.x]).astype(jnp.int32)
    anywhere = pl.BlockSpec(memory_space=pl.ANY)
    outs = pl.pallas_call(
        functools.partial(join_kernel, quarters=quarters, split=split),
        in_specs=[pl.BlockSpec(memory_space=pltpu.SMEM)] + [anywhere] * len(refs),
        out_specs=[pl.BlockSpec(memory_space=pltpu.VMEM)] * len(quarters),
        out_shape=[jax.ShapeDtypeStruct((8, 4, q, columns), BF) for q in quarters],
        scratch_shapes=[pltpu.SemaphoreType.DMA((24 * len(quarters),))],
        compiler_params=pltpu.CompilerParams(vmem_limit_bytes=48 << 20),
        name="join",
    )(place, *refs)
    return [out.reshape(32 * q, columns) for out, q in zip(outs, quarters)]


def scatter_task(links, grads, split):
    columns = grads[0].shape[1]
    quarters = [grad.shape[0] // 32 for grad in grads]
    whole = [grad.reshape(8, 4, q, columns) for grad, q in zip(grads, quarters)]

    def half(which):
        parts = [take(item, 2 * which, 2, 1) for item in whole]
        return parts[0] if len(parts) == 1 else jnp.concatenate(parts, axis=2)

    got = links.swap(half(1 - links.core), links.CORE)
    (got,) = yield (got,)
    both = (half(links.core) + got).reshape(4, 2, 2, sum(quarters), columns)
    other = take(both, 1 - links.y, 1, 1)[:, 0]
    own = take(both, links.y, 1, 1)[:, 0]
    if split:
        got = links.swap(take(other, 1 - links.x, 1, 1), links.X)
        own, other, got = yield (own, other, got)
        other = links.swap(take(other, links.x, 1, 1) + got, links.Y)
        own, other = yield (own, other)
        own = lax.dynamic_update_slice_in_dim(own, take(own, links.x, 1, 1) + other, links.x, 1)
    else:
        other = links.swap(other, links.Y)
        own, other = yield (own, other)
        own = own + other

    def at(bits):
        return take(own, links.z ^ bits, 1, 0)[0]

    second = links.swap(at(2), links.Z1)
    own, second = yield (own, second)
    far = links.swap(at(3) + second, links.Z3)
    near = links.swap(at(1), links.Z1)
    own, near, far = yield (own, near, far)
    total = at(0) + near + far
    got = links.swap(total, links.X)
    total, got = yield (total, got)
    total = total + got
    twin = links.swap(total, links.CORE)
    total, twin = yield (total, twin)
    total = jnp.where(
        links.core == 0,
        jnp.concatenate([total, twin], axis=0),
        jnp.concatenate([twin, total], axis=0),
    ).astype(F32)
    results = []
    offset = 0
    for q in quarters:
        results.append(total[:, offset : offset + q].reshape(4 * q, columns))
        offset += q
    return results


def plain_gather_task(pieces):
    yield ()
    return [lax.all_gather(piece, "fsdp", axis=0, tiled=True) for piece in pieces]


def plain_scatter_task(grads):
    yield ()
    return [
        lax.psum(lax.psum_scatter(grad, "fsdp", scatter_dimension=0, tiled=True), "grp").astype(F32)
        for grad in grads
    ]


class Ticks:
    def __init__(self):
        self.tasks = {}
        self.held = {}
        self.done = {}

    def add(self, name, task):
        self.tasks[name] = task

    def advance(self, name):
        task = self.tasks[name]
        try:
            self.held[name] = task.send(self.held.pop(name)) if name in self.held else next(task)
        except StopIteration as end:
            self.done[name] = end.value
            del self.tasks[name]

    def tick(self, names, compute=None):
        for name in names:
            if name in self.tasks:
                self.advance(name)
        made = compute() if compute else ()
        made, self.held = lax.optimization_barrier((made, self.held))
        return made

    def result(self, name):
        while name in self.tasks:
            self.advance(name)
        return self.done[name]


def pack_gains(gains):
    rows = jnp.stack(gains)
    width = 1024
    return jnp.pad(rows[:, None], ((0, 0), (0, GAIN_ROWS - 1), (0, width - rows.shape[1]))).reshape(
        4 * GAIN_ROWS, width
    )


def unpack_gains(rows, shards, size):
    rows = rows.reshape(shards, 4, GAIN_ROWS, -1)[:, :, 0, :size]
    return [rows[:, j].reshape(shards * size).astype(F32) for j in range(4)]


def pack_gain_grads(grads, shards):
    rows = jnp.stack([grad.reshape(shards, -1) for grad in grads], axis=1).astype(BF)
    return jnp.pad(
        rows[:, :, None], ((0, 0), (0, 0), (0, GAIN_ROWS - 1), (0, 1024 - rows.shape[2]))
    ).reshape(shards * 4 * GAIN_ROWS, 1024)


def matmul(left, right, left_dim, right_dim, kind=F32):
    return dot(left, right, left_dim, right_dim).astype(kind)


def body(
    latent_state,
    prelude_embed,
    out_grad,
    piece_starts,
    w_adapter,
    w_query,
    w_key,
    w_value,
    w_out,
    w_gate,
    w_up,
    w_down,
    gain_attn_in,
    gain_attn_out,
    gain_ffn_in,
    gain_ffn_out,
    *,
    shards,
    linked,
):
    links = Links() if linked else None
    seq_count, length, width = latent_state.shape
    pairs = width // PAIR
    per_call = pairs // 4
    ticks = Ticks()

    def gather(name, pieces, split):
        ticks.add(name, gather_task(links, pieces, split) if linked else plain_gather_task(pieces))

    def scatter(name, grads, split):
        ticks.add(name, scatter_task(links, grads, split) if linked else plain_scatter_task(grads))

    gains = pack_gains([gain_attn_in, gain_attn_out, gain_ffn_in, gain_ffn_out])
    gather("A", [w_adapter], False)
    gather("B", [w_query, w_key, gains], False)
    gather("V", [w_value, w_out], False)
    gather("G", [w_gate], True)
    gather("U", [w_up], True)
    gather("D", [w_down], True)
    state = latent_state.reshape(length, width)
    embed = prelude_embed.reshape(length, width)
    grad_rows = out_grad.reshape(length, width)
    tick = ticks.tick
    tick(["A"])
    tick(["A", "B"])
    tick(["A", "B", "V"])
    tick(["A", "B", "V", "G"])
    (adapter,) = ticks.result("A")
    tables = rotary_tables(length)

    def first():
        return (
            matmul(state, adapter[:width], 1, 0) + matmul(embed, adapter[width:], 1, 0),
            *tables,
        )

    hidden, cosine, sine = tick(["B", "V", "G", "U"], first)
    wq, wk, gains = ticks.result("B")
    gain_one, gain_two, gain_three, gain_four = unpack_gains(gains, shards, gain_attn_in.shape[0])

    def projections():
        normed = rms_parts(hidden, gain_one)[0].astype(BF)
        return normed, matmul(normed, wq, 1, 0), matmul(normed, wk, 1, 0)

    normed, query, key = tick(["V", "G", "U", "D"], projections)
    wv, wo = ticks.result("V")
    value = matmul(normed, wv, 1, 0, BF)
    results = None
    for i, names in enumerate((["G", "U", "D"], ["G", "U", "D"], ["U", "D"], ["D"])):
        results = tick(
            names,
            lambda: attention_forward(
                piece_starts, query, key, value, cosine, sine, per_call, i * per_call, results
            ),
        )
    attended, query_rot, key_rot, lse = results
    (gate_w,) = ticks.result("G")
    (up_w,) = ticks.result("U")

    def feed_in():
        branch = matmul(attended, wo, 1, 0)
        mixed = hidden + rms_parts(branch, gain_two)[0]
        ffn_in = rms_parts(mixed, gain_three)[0].astype(BF)
        gate = matmul(ffn_in, gate_w, 1, 0)
        up_value = matmul(ffn_in, up_w, 1, 0)
        product = (gate * jax.nn.sigmoid(gate) * up_value).astype(BF)
        return branch, mixed, ffn_in, gate, up_value, product

    branch, mixed, ffn_in, gate, up_value, product = tick(["D"], feed_in)
    (down_w,) = ticks.result("D")

    def feed_out():
        ffn_out = matmul(product, down_w, 1, 0)
        ffn_normed, inverse = rms_parts(ffn_out, gain_four)
        block_output = (mixed + ffn_normed).astype(BF).reshape(seq_count, length, width)
        ffn_grad, gain_four_grad = norm_back(ffn_out, inverse, gain_four, grad_rows.astype(F32))
        ffn_grad = ffn_grad.astype(BF)
        return block_output, ffn_grad, gain_four_grad, matmul(product, ffn_grad, 0, 0, BF)

    block_output, ffn_grad, gain_four_grad, down_grad = tick([], feed_out)
    scatter("down", [down_grad], True)

    def product_back():
        product_grad = matmul(ffn_grad, down_w, 1, 1)
        sigmoid_gate = jax.nn.sigmoid(gate)
        gate_grad = product_grad * up_value * (sigmoid_gate * (1.0 + gate * (1.0 - sigmoid_gate)))
        return gate_grad.astype(BF), (product_grad * (gate * sigmoid_gate)).astype(BF)

    gate_grad, up_grad = tick(["down"], product_back)
    (gate_weight_grad,) = tick(["down"], lambda: (matmul(ffn_in, gate_grad, 0, 0, BF),))
    scatter("gate", [gate_weight_grad], True)
    (up_weight_grad,) = tick(["down", "gate"], lambda: (matmul(ffn_in, up_grad, 0, 0, BF),))
    scatter("up", [up_weight_grad], True)

    def ffn_back():
        return (matmul(gate_grad, gate_w, 1, 1) + matmul(up_grad, up_w, 1, 1),)

    (ffn_in_grad,) = tick(["down", "gate", "up"], ffn_back)

    def branch_back():
        inverse = rms_parts(mixed, gain_three)[1]
        mixed_part, gain_three_grad = norm_back(mixed, inverse, gain_three, ffn_in_grad)
        mixed_grad = grad_rows.astype(F32) + mixed_part
        inverse = rms_parts(branch, gain_two)[1]
        branch_grad, gain_two_grad = norm_back(branch, inverse, gain_two, mixed_grad)
        branch_grad = branch_grad.astype(BF)
        return (
            mixed_grad,
            gain_two_grad,
            gain_three_grad,
            matmul(attended, branch_grad, 0, 0, BF),
            matmul(branch_grad, wo, 1, 1, BF),
        )

    mixed_grad, gain_two_grad, gain_three_grad, out_weight_grad, attended_grad = tick(
        ["down", "gate", "up"], branch_back
    )
    scatter("out", [out_weight_grad], False)
    results = None
    for i in range(4):
        results = tick(
            ["down", "gate", "up", "out"],
            lambda: attention_backward(
                piece_starts, query_rot, key_rot, value, attended_grad, attended, lse, cosine, sine,
                per_call, i * per_call, results,
            ),
        )
    query_grad, key_grad, value_grad = results

    def projection_grads():
        return (
            matmul(normed, query_grad, 0, 0, BF),
            matmul(normed, key_grad, 0, 0, BF),
            matmul(normed, value_grad, 0, 0, BF),
        )

    grads = tick(["gate", "up", "out"], projection_grads)
    scatter("qkv", list(grads), False)

    def hidden_back():
        normed_grad = (
            matmul(query_grad, wq, 1, 1) + matmul(key_grad, wk, 1, 1) + matmul(value_grad, wv, 1, 1)
        )
        inverse = rms_parts(hidden, gain_one)[1]
        hidden_part, gain_one_grad = norm_back(hidden, inverse, gain_one, normed_grad)
        return (mixed_grad + hidden_part).astype(BF), gain_one_grad

    hidden_grad, gain_one_grad = tick(["up", "out", "qkv"], hidden_back)

    def adapter_back():
        gain_grads = pack_gain_grads(
            [gain_one_grad, gain_two_grad, gain_three_grad, gain_four_grad], shards
        )
        adapter_grad = jnp.concatenate(
            [matmul(state, hidden_grad, 0, 0, BF), matmul(embed, hidden_grad, 0, 0, BF)], axis=0
        )
        return adapter_grad, gain_grads

    adapter_grad, gain_grads = tick(["out", "qkv"], adapter_back)
    scatter("adapter", [adapter_grad, gain_grads], False)

    def joined_back():
        return (
            matmul(hidden_grad, adapter[:width], 1, 1, BF).reshape(seq_count, length, width),
            matmul(hidden_grad, adapter[width:], 1, 1, BF).reshape(seq_count, length, width),
        )

    state_grad, embed_grad = tick(["qkv", "adapter"], joined_back)
    while "adapter" in ticks.tasks or "qkv" in ticks.tasks:
        tick(["qkv", "adapter"])
    adapter_grad, gain_grads = ticks.result("adapter")
    gain_grads = unpack_gains(gain_grads, 1, gain_attn_in.shape[0])
    return (
        block_output,
        state_grad,
        embed_grad,
        adapter_grad,
        *ticks.result("qkv"),
        *ticks.result("out"),
        *ticks.result("gate"),
        *ticks.result("up"),
        *ticks.result("down"),
        *gain_grads,
    )


def solution(mesh):
    rows = P(("grp", "fsdp"), None, None)
    matrix = P("fsdp", None)
    vector = P("fsdp")
    in_specs = (rows,) * 3 + (P(("grp", "fsdp"), None),) + (matrix,) * 8 + (vector,) * 4
    out_specs = (rows,) * 3 + (matrix,) * 8 + (vector,) * 4
    shards = mesh.shape["fsdp"]
    linked = (mesh.shape["grp"], shards) == (4, 8)
    return jax.shard_map(
        functools.partial(body, shards=shards, linked=linked),
        mesh=mesh,
        in_specs=in_specs,
        out_specs=out_specs,
        check_vma=False,
    )
```

```python
import functools

import jax
import jax.numpy as jnp
from jax import lax
from jax.experimental import pallas as pl
from jax.experimental.pallas import tpu as pltpu
from jax.sharding import PartitionSpec as P

HEAD_DIM = 64
PIECE = 256
PAIR = 2 * HEAD_DIM
GAIN_ROWS = 8
TILE = 256
MIB = 1 << 20

EPS = 1e-06
NEG = -1e30
THETA = 50000.0
AXES = ("grp", "fsdp")
F32 = jnp.float32
BF = jnp.bfloat16


def dot(left, right, left_dim, right_dim):
    return lax.dot_general(
        left, right, (((left_dim,), (right_dim,)), ((), ())), preferred_element_type=F32
    )


def inverse_rms(value):
    return lax.rsqrt(jnp.mean(value * value, axis=-1, keepdims=True) + EPS)


def norm_back(value, inverse, gain, grad_out):
    scaled = gain * grad_out
    unit = value * inverse
    gain_grad = jnp.sum(grad_out * unit, axis=0, keepdims=True)
    mean = jnp.mean(scaled * unit, axis=-1, keepdims=True)
    return inverse * (scaled - unit * mean), gain_grad


def bias_kernel(starts_ref, bias_ref):
    rows, length = bias_ref.shape
    key_pos = lax.broadcasted_iota(jnp.int32, (rows, length), 0) + pl.program_id(0) * rows
    query_pos = lax.broadcasted_iota(jnp.int32, (rows, length), 1)
    allowed = key_pos <= query_pos
    for k in range(2):
        first = starts_ref[0, k]
        last = first + PIECE
        allowed = allowed | (
            (key_pos >= first) & (key_pos < last) & (query_pos >= first) & (query_pos < last)
        )
    bias_ref[...] = jnp.where(allowed, 0.0, NEG).astype(BF)


def make_bias(starts, length):
    rows = 128
    return pl.pallas_call(
        bias_kernel,
        grid=(length // rows,),
        in_specs=[pl.BlockSpec(memory_space=pltpu.SMEM)],
        out_specs=pl.BlockSpec((rows, length), lambda i: (i, 0)),
        out_shape=jax.ShapeDtypeStruct((length, length), BF),
        name="bias",
    )(starts)


def swap_halves(values):
    width = values.shape[1]
    half = HEAD_DIM // 2
    lane = lax.broadcasted_iota(jnp.int32, values.shape, 1)
    return jnp.where(
        (lane % HEAD_DIM) < half,
        pltpu.roll(values, width - half, 1),
        pltpu.roll(values, half, 1),
    )


def extents(length, rows):
    slot = length // 2
    return [(lo, ((lo + rows - 1) // slot + 1) * slot) for lo in range(0, length, rows)]


def add_bias(scores, bias_ref, lo, hi, rows):
    bias = bias_ref[lo:hi, lo : lo + rows].astype(F32)
    if lo == 0:
        return scores + bias
    return jnp.concatenate([scores[:lo], scores[lo:] + bias], axis=0)


def only(array, a):
    low = lax.broadcasted_iota(jnp.int32, array.shape, 1) < HEAD_DIM
    zero = BF(0)
    return jnp.where(low, array, zero) if a == 0 else jnp.where(low, zero, array)


def forward_kernel(bias_ref, q_ref, k_ref, v_ref, o_ref, lse_ref, *, length, rows):
    query_rot = q_ref[...]
    key_rot = k_ref[...]
    value_t = v_ref[...].T
    keys = (only(key_rot, 0), only(key_rot, 1))
    for lo, hi in extents(length, rows):
        block = query_rot[lo : lo + rows]
        outs = []
        for a in range(2):
            scores = add_bias(dot(keys[a][:hi], block, 1, 1), bias_ref, lo, hi, rows)
            top = jnp.max(scores, axis=0, keepdims=True)
            exponent = jnp.exp(scores - top)
            total = jnp.sum(exponent, axis=0, keepdims=True)
            lse_ref[0, a : a + 1, lo : lo + rows] = top + jnp.log(total)
            head = value_t[HEAD_DIM * a : HEAD_DIM * (a + 1), :hi]
            outs.append(dot(head, exponent.astype(BF), 1, 0) * (1.0 / total))
        o_ref[lo : lo + rows, :] = jnp.concatenate(outs, 0).T.astype(BF)


def backward_kernel(
    bias_ref, q_ref, k_ref, v_ref, g_ref, o_ref, lse_ref, cos_ref, sin_ref,
    dq_ref, dk_ref, dv_ref, *, length, rows
):
    query_rot = q_ref[...]
    key_rot = k_ref[...]
    value = v_ref[...]
    grad = g_ref[...]
    keys = (only(key_rot, 0), only(key_rot, 1))
    values = (only(value, 0), only(value, 1))
    key_t = key_rot.T
    product = grad.astype(F32) * o_ref[...].astype(F32)
    key_grad = jnp.zeros((length, PAIR), F32)
    value_grad = jnp.zeros((length, PAIR), F32)
    cosine = cos_ref[...]
    sine = sin_ref[...]

    def turn_back(array, lo, count):
        return array * cosine[lo : lo + count] - swap_halves(array) * sine[lo : lo + count]

    def add_rows(total, part, hi):
        if hi == length:
            return total + part
        return jnp.concatenate([total[:hi] + part, total[hi:]], axis=0)

    for lo, hi in extents(length, rows):
        query_block = query_rot[lo : lo + rows]
        grad_block = grad[lo : lo + rows]
        product_t = product[lo : lo + rows].T
        parts = []
        for a in range(2):
            delta = jnp.sum(product_t[HEAD_DIM * a : HEAD_DIM * (a + 1)], axis=0, keepdims=True)
            scores = dot(keys[a][:hi], query_block, 1, 1) - lse_ref[0, a : a + 1, lo : lo + rows]
            probs = jnp.exp(add_bias(scores, bias_ref, lo, hi, rows))
            probs_grad = dot(values[a][:hi], grad_block, 1, 1)
            score_grad = (probs * (probs_grad - delta)).astype(BF)
            value_grad = add_rows(value_grad, dot(probs.astype(BF), only(grad_block, a), 1, 0), hi)
            key_grad = add_rows(key_grad, dot(score_grad, only(query_block, a), 1, 0), hi)
            parts.append(dot(key_t[HEAD_DIM * a : HEAD_DIM * (a + 1), :hi], score_grad, 1, 0))
        query_grad = (jnp.concatenate(parts, 0) * HEAD_DIM**-0.5).T
        dq_ref[lo : lo + rows, :] = turn_back(query_grad, lo, rows).astype(BF)
    dk_ref[...] = turn_back(key_grad, 0, length).astype(BF)
    dv_ref[...] = value_grad.astype(BF)


def rotary_tables(length):
    half = HEAD_DIM // 2
    position = jnp.arange(length, dtype=F32)
    frequency = THETA ** (-jnp.arange(half, dtype=F32) / half)
    angles = position[:, None] * frequency[None, :]
    cosine, sine = jnp.cos(angles), jnp.sin(angles)
    return (
        jnp.concatenate([cosine] * 4, axis=1),
        jnp.concatenate([-sine, sine, -sine, sine], axis=1),
    )


def without_refs(kernel, place, count):
    def run(*refs):
        return kernel(*refs[:place], *refs[place + count :])

    return run


def attention_specs(length, first):
    square = pl.BlockSpec((length, length), lambda i: (0, 0), pipeline_mode=pl.Buffered(1))
    column = pl.BlockSpec((length, PAIR), lambda i: (0, i + first))
    table = pl.BlockSpec((length, PAIR), lambda i: (0, 0))
    sums = pl.BlockSpec((1, 2, length), lambda i: (i + first, 0, 0))
    return square, column, table, sums


def attention_call(kernel, name, steps, inputs, in_specs, out_specs, out_shape, earlier):
    anywhere = pl.BlockSpec(memory_space=pl.ANY)
    count = len(inputs)
    earlier = list(earlier or ())
    return pl.pallas_call(
        without_refs(kernel, count, len(earlier)),
        grid=(steps,),
        in_specs=in_specs + [anywhere] * len(earlier),
        out_specs=out_specs,
        out_shape=out_shape,
        input_output_aliases={count + i: i for i in range(len(earlier))},
        compiler_params=pltpu.CompilerParams(vmem_limit_bytes=48 * MIB),
        cost_estimate=pl.CostEstimate(
            flops=steps * 2_000_000_000, transcendentals=steps * 2 * MIB, bytes_accessed=steps * 2 * MIB
        ),
        name=name,
    )(*inputs, *earlier)


def attention_forward(bias, query_rot, key_rot, value, steps, first, earlier, rows=512):
    length, width = query_rot.shape
    square, column, table, sums = attention_specs(length, first)
    return attention_call(
        functools.partial(forward_kernel, length=length, rows=rows),
        "attention_forward",
        steps,
        [bias, query_rot, key_rot, value],
        [square, column, column, column],
        [column, sums],
        [
            jax.ShapeDtypeStruct((length, width), BF),
            jax.ShapeDtypeStruct((width // PAIR, 2, length), F32),
        ],
        earlier,
    )


def attention_backward(
    bias, query_rot, key_rot, value, grad, attended, lse, cosine, sine, steps, first, earlier, rows=256
):
    length, width = query_rot.shape
    square, column, table, sums = attention_specs(length, first)
    half = jax.ShapeDtypeStruct((length, width), BF)
    return attention_call(
        functools.partial(backward_kernel, length=length, rows=rows),
        "attention_backward",
        steps,
        [bias, query_rot, key_rot, value, grad, attended, lse, cosine, sine],
        [square, column, column, column, column, column, sums, table, table],
        [column, column, column],
        [half, half, half],
        earlier,
    )


class Links:
    X, CORE, Z1, Z3, Y = 16, 8, 2, 6, 1

    def __init__(self):
        group = lax.axis_index("grp")
        shard = lax.axis_index("fsdp")
        self.x, self.core = group // 2, group % 2
        self.z, self.y = shard // 2, shard % 2

    def swap(self, value, bits):
        return lax.ppermute(value, AXES, [(d, d ^ bits) for d in range(32)])


def take(value, start, size, axis):
    return lax.dynamic_slice_in_dim(value, start, size, axis)


class Pieces:
    def __init__(self, arrays, offset, size, shape, split, columns, place):
        self.arrays, self.offset, self.size = arrays, offset, size
        self.shape, self.split, self.columns, self.place = shape, split, columns, place

    def copies(self, place_ref, refs, target):
        if self.place is None:
            return [(refs[0], target)]
        z, y, core, x = (place_ref[i] for i in range(4))
        zs, zc, ry, yc = refs[:4]
        part = pl.ds(self.offset, self.size)
        pairs = []

        def spot(row, column, j):
            shard = 2 * row + column
            if self.columns:
                rows, width = self.size, self.shape[1] // 4
                return target.at[
                    pl.ds(pl.multiple_of(shard * rows, 8), rows),
                    pl.ds(pl.multiple_of(j * width, 128), width),
                ]
            return target.at[
                pl.ds(pl.multiple_of((shard * 4 + j) * self.size, self.size), self.size), :
            ]

        for r in range(4):
            row = z ^ r
            for k in range(2):
                pairs.append((zs.at[r, k, part], spot(row, y, 2 * core + k)))
                pairs.append((zc.at[r, k, part], spot(row, y, 2 - 2 * core + k)))
                if not self.split:
                    pairs.append((ry.at[r, k, part], spot(row, 1 - y, 2 * core + k)))
                    pairs.append((yc.at[r, k, part], spot(row, 1 - y, 2 - 2 * core + k)))
            if self.split:
                rx, xc = refs[4:6]
                pairs.append((ry.at[r, part], spot(row, 1 - y, 2 * core + x)))
                pairs.append((rx.at[r, part], spot(row, 1 - y, 2 * core + 1 - x)))
                pairs.append((yc.at[r, part], spot(row, 1 - y, 2 - 2 * core + x)))
                pairs.append((xc.at[r, part], spot(row, 1 - y, 3 - 2 * core - x)))
        return pairs


def row_call(kernel, name, length, tiles, fulls, weights, outs, sums=0, keep=(), flops=0):
    places = [w.place for w in weights if w.place is not None]
    scalars = places[:1]
    anywhere = pl.BlockSpec(memory_space=pl.ANY)
    arrays = []
    spans = []
    for weight in weights:
        known = [i for i, span in enumerate(spans) if arrays[span[0]] is weight.arrays[0]]
        if known:
            spans.append(spans[known[0]])
        else:
            spans.append((len(arrays), len(arrays) + len(weight.arrays)))
            arrays += weight.arrays
    total = sum(32 if w.place is not None else 1 for w in weights)
    steps = length // TILE

    def run(*refs):
        refs = list(refs)

        def pull(count):
            taken = refs[:count]
            del refs[:count]
            return taken

        place_ref = pull(len(scalars))
        tile_refs, full_refs, array_refs = pull(len(tiles)), pull(len(fulls)), pull(len(arrays))
        out_refs, sum_refs, keep_refs = pull(len(outs)), pull(sums), pull(len(keep))
        weight_refs = pull(len(weights))
        load_sems, keep_sems = pull(2) if weights else (None, None)
        step = pl.program_id(0)

        def kept(i):
            return pltpu.make_async_copy(weight_refs[keep[i]], keep_refs[i], keep_sems.at[i])

        if weights:

            @pl.when(step == 0)
            def _():
                loads = []
                for weight, (lo, hi), target in zip(weights, spans, weight_refs):
                    where = place_ref[0] if place_ref else None
                    for source, spot in weight.copies(where, array_refs[lo:hi], target):
                        loads.append(pltpu.make_async_copy(source, spot, load_sems.at[len(loads)]))
                        loads[-1].start()
                for load in loads:
                    load.wait()
                for i in range(len(keep)):
                    kept(i).start()

        if sums:

            @pl.when(step == 0)
            def _():
                for ref in sum_refs:
                    ref[...] = jnp.zeros_like(ref)

        kernel(tile_refs, full_refs, weight_refs, out_refs, sum_refs)
        if keep:

            @pl.when(step == steps - 1)
            def _():
                for i in range(len(keep)):
                    kept(i).wait()

    def whole(array):
        return pl.BlockSpec(array.shape, lambda i: (0, 0), pipeline_mode=pl.Buffered(1))

    moved = sum(a.size * a.dtype.itemsize for a in list(tiles) + list(fulls) + arrays)
    return pl.pallas_call(
        run,
        grid=(steps,),
        in_specs=[pl.BlockSpec(memory_space=pltpu.SMEM)] * len(scalars)
        + [pl.BlockSpec((TILE, a.shape[1]), lambda i: (i, 0)) for a in tiles]
        + [whole(a) for a in fulls]
        + [anywhere] * len(arrays),
        out_specs=[pl.BlockSpec((TILE, n), lambda i: (i, 0)) for n, _ in outs]
        + [pl.BlockSpec((1, 1024), lambda i: (0, 0))] * sums
        + [anywhere] * len(keep),
        out_shape=[jax.ShapeDtypeStruct((length, n), kind) for n, kind in outs]
        + [jax.ShapeDtypeStruct((1, 1024), F32)] * sums
        + [jax.ShapeDtypeStruct(weights[i].shape, BF) for i in keep],
        scratch_shapes=[pltpu.VMEM(w.shape, BF) for w in weights]
        + (
            [pltpu.SemaphoreType.DMA((total,)), pltpu.SemaphoreType.DMA((max(len(keep), 1),))]
            if weights
            else []
        ),
        compiler_params=pltpu.CompilerParams(vmem_limit_bytes=56 * MIB),
        cost_estimate=pl.CostEstimate(
            flops=flops * length, transcendentals=length * 1024, bytes_accessed=moved
        ),
        name=name,
    )(*scalars, *tiles, *fulls, *arrays)


def gather_task(links, pieces, split, columns=False):
    width = pieces[0].shape[1]
    if columns:
        (piece,) = pieces
        sizes = [piece.shape[0]]
        packed = piece.reshape(piece.shape[0], 4, width // 4).transpose(1, 0, 2)
    else:
        sizes = [piece.shape[0] // 4 for piece in pieces]
        packed = [piece.reshape(4, -1, width) for piece in pieces]
        packed = packed[0] if len(packed) == 1 else jnp.concatenate(packed, axis=1)
    mine = take(packed, 2 * links.core, 2, 0)
    far = links.swap(mine, links.Z3)
    near = links.swap(mine, links.Z1)
    mine, near, far = yield (mine, near, far)
    second = links.swap(far, links.Z1)
    (second,) = yield (second,)
    zs = jnp.stack([mine, near, second, far])
    ry = links.swap(take(zs, links.x, 1, 1)[:, 0] if split else zs, links.Y)
    zs, ry = yield (zs, ry)
    parts = [zs, ry]
    if split:
        rx = links.swap(ry, links.X)
        (rx,) = yield (rx,)
        parts.append(rx)
    twins = [links.swap(item, links.CORE) for item in parts]
    twins = yield tuple(twins)
    arrays = [item for pair in zip(parts, twins) for item in pair]
    place = jnp.stack([links.z, links.y, links.core, links.x]).astype(jnp.int32)
    results = []
    offset = 0
    for piece, size in zip(pieces, sizes):
        shape = (8 * piece.shape[0], width)
        results.append(Pieces(arrays, offset, size, shape, split, columns, place))
        offset += size
    return results


def scatter_task(links, grads, split):
    columns = grads[0].shape[1]
    quarters = [grad.shape[0] // 32 for grad in grads]
    whole = [grad.reshape(8, 4, q, columns) for grad, q in zip(grads, quarters)]

    def half(which):
        parts = [take(item, 2 * which, 2, 1) for item in whole]
        return parts[0] if len(parts) == 1 else jnp.concatenate(parts, axis=2)

    got = links.swap(half(1 - links.core), links.CORE)
    (got,) = yield (got,)
    both = (half(links.core) + got).reshape(4, 2, 2, sum(quarters), columns)
    other = take(both, 1 - links.y, 1, 1)[:, 0]
    own = take(both, links.y, 1, 1)[:, 0]
    if split:
        got = links.swap(take(other, 1 - links.x, 1, 1), links.X)
        own, other, got = yield (own, other, got)
        other = links.swap(take(other, links.x, 1, 1) + got, links.Y)
        own, other = yield (own, other)
        own = lax.dynamic_update_slice_in_dim(own, take(own, links.x, 1, 1) + other, links.x, 1)
    else:
        other = links.swap(other, links.Y)
        own, other = yield (own, other)
        own = own + other

    def at(bits):
        return take(own, links.z ^ bits, 1, 0)[0]

    second = links.swap(at(2), links.Z1)
    own, second = yield (own, second)
    far = links.swap(at(3) + second, links.Z3)
    near = links.swap(at(1), links.Z1)
    own, near, far = yield (own, near, far)
    total = at(0) + near + far
    got = links.swap(total, links.X)
    total, got = yield (total, got)
    total = total + got
    twin = links.swap(total, links.CORE)
    total, twin = yield (total, twin)
    total = jnp.where(
        links.core == 0,
        jnp.concatenate([total, twin], axis=0),
        jnp.concatenate([twin, total], axis=0),
    ).astype(F32)
    results = []
    offset = 0
    for q in quarters:
        results.append(total[:, offset : offset + q].reshape(4 * q, columns))
        offset += q
    return results


def plain_gather_task(pieces):
    yield ()
    full = [lax.all_gather(piece, "fsdp", axis=0, tiled=True) for piece in pieces]
    return [Pieces([item], 0, 0, item.shape, False, False, None) for item in full]


def plain_scatter_task(grads):
    yield ()
    return [
        lax.psum(lax.psum_scatter(grad, "fsdp", scatter_dimension=0, tiled=True), "grp").astype(F32)
        for grad in grads
    ]


class Ticks:
    def __init__(self):
        self.tasks = {}
        self.held = {}
        self.done = {}

    def add(self, name, task):
        self.tasks[name] = task

    def advance(self, name):
        task = self.tasks[name]
        try:
            self.held[name] = task.send(self.held.pop(name)) if name in self.held else next(task)
        except StopIteration as end:
            self.done[name] = end.value
            del self.tasks[name]

    def tick(self, names, compute=None):
        for name in names:
            if name in self.tasks:
                self.advance(name)
        made = compute() if compute else ()
        made, self.held = lax.optimization_barrier((made, self.held))
        return made

    def result(self, name):
        while name in self.tasks:
            self.advance(name)
        return self.done[name]


def pack_gains(gains):
    rows = jnp.stack(gains)
    width = 1024
    return jnp.pad(rows[:, None], ((0, 0), (0, GAIN_ROWS - 1), (0, width - rows.shape[1]))).reshape(
        4 * GAIN_ROWS, width
    )


def join_kernel(place_ref, *refs, weight):
    out, sems = refs[-2:]
    copies = []
    for source, spot in weight.copies(place_ref, refs[:-2], out):
        copies.append(pltpu.make_async_copy(source, spot, sems.at[len(copies)]))
        copies[-1].start()
    for item in copies:
        item.wait()


def join(weight):
    if weight.place is None:
        return weight.arrays[0]
    return pl.pallas_call(
        functools.partial(join_kernel, weight=weight),
        in_specs=[pl.BlockSpec(memory_space=pltpu.SMEM)]
        + [pl.BlockSpec(memory_space=pl.ANY)] * len(weight.arrays),
        out_specs=pl.BlockSpec(memory_space=pltpu.VMEM),
        out_shape=jax.ShapeDtypeStruct(weight.shape, BF),
        scratch_shapes=[pltpu.SemaphoreType.DMA((32,))],
        name="join",
    )(weight.place, *weight.arrays)


def unpack_gains(rows, shards, size):
    rows = rows.reshape(shards, 4, GAIN_ROWS, -1)[:, :, 0, :size]
    return [rows[:, j].reshape(shards * size).astype(F32) for j in range(4)]


def pack_gain_grads(grads, shards):
    rows = jnp.stack([grad.reshape(shards, -1) for grad in grads], axis=1).astype(BF)
    return jnp.pad(
        rows[:, :, None], ((0, 0), (0, 0), (0, GAIN_ROWS - 1), (0, 1024 - rows.shape[2]))
    ).reshape(shards * 4 * GAIN_ROWS, 1024)


def matmul(left, right, left_dim, right_dim, kind=F32):
    return dot(left, right, left_dim, right_dim).astype(kind)


def hidden_rows(tiles, fulls, weights, outs, sums):
    state, embed = tiles
    (adapter,) = weights
    width = state.shape[1]
    outs[0][...] = dot(state[...], adapter[:width, :], 1, 0) + dot(
        embed[...], adapter[width:, :], 1, 0
    )


def projection_rows(tiles, fulls, weights, outs, sums):
    hidden_ref, cos_ref, sin_ref = tiles
    (gains,) = fulls
    normed_ref, query_ref, key_ref, value_ref = outs
    hidden = hidden_ref[...]
    normed = (hidden * inverse_rms(hidden) * gains[0:1, :]).astype(BF)
    normed_ref[...] = normed
    cosine, sine = cos_ref[...], sin_ref[...]
    for weight, out, scale in ((weights[0], query_ref, HEAD_DIM**-0.5), (weights[1], key_ref, None)):
        flat = dot(normed, weight[...], 1, 0)
        for lo in range(0, flat.shape[1], PAIR):
            part = flat[:, lo : lo + PAIR]
            turned = (part * cosine + swap_halves(part) * sine).astype(BF)
            out[:, lo : lo + PAIR] = turned if scale is None else turned * BF(scale)
    value_ref[...] = dot(normed, weights[2][...], 1, 0).astype(BF)


def feed_in_rows(tiles, fulls, weights, outs, sums):
    attended, hidden = tiles
    (gains,) = fulls
    wo, gate_w, up_w = weights
    branch_ref, mixed_ref, ffn_in_ref, gate_ref, up_ref, product_ref = outs
    branch = dot(attended[...], wo[...], 1, 0)
    branch_ref[...] = branch
    mixed = hidden[...] + branch * inverse_rms(branch) * gains[1:2, :]
    mixed_ref[...] = mixed
    ffn_in = (mixed * inverse_rms(mixed) * gains[2:3, :]).astype(BF)
    ffn_in_ref[...] = ffn_in
    gate = dot(ffn_in, gate_w[...], 1, 0)
    gate_ref[...] = gate.astype(BF)
    up_value = dot(ffn_in, up_w[...], 1, 0)
    up_ref[...] = up_value.astype(BF)
    product_ref[...] = (gate * jax.nn.sigmoid(gate) * up_value).astype(BF)


def feed_out_rows(tiles, fulls, weights, outs, sums):
    product, mixed, grad_rows, gate_ref, up_ref = tiles
    (gains,) = fulls
    (down_w,) = weights
    block_ref, ffn_grad_ref, gate_grad_ref, up_grad_ref = outs
    gain = gains[3:4, :]
    ffn_out = dot(product[...], down_w[...], 1, 0)
    inverse = inverse_rms(ffn_out)
    block_ref[...] = (mixed[...] + ffn_out * inverse * gain).astype(BF)
    ffn_grad, gain_grad = norm_back(ffn_out, inverse, gain, grad_rows[...].astype(F32))
    sums[0][...] += gain_grad
    ffn_grad = ffn_grad.astype(BF)
    ffn_grad_ref[...] = ffn_grad
    product_grad = dot(ffn_grad, down_w[...], 1, 1)
    gate = gate_ref[...].astype(F32)
    sigmoid_gate = jax.nn.sigmoid(gate)
    gate_grad_ref[...] = (
        product_grad
        * up_ref[...].astype(F32)
        * (sigmoid_gate * (1.0 + gate * (1.0 - sigmoid_gate)))
    ).astype(BF)
    up_grad_ref[...] = (product_grad * (gate * sigmoid_gate)).astype(BF)


def feed_back_rows(tiles, fulls, weights, outs, sums):
    gate_grad, up_grad, mixed_ref, branch_ref, grad_rows = tiles
    gains, gate_w, up_w, wo = fulls
    mixed_grad_ref, branch_grad_ref, attended_grad_ref = outs
    ffn_in_grad = dot(gate_grad[...], gate_w[...], 1, 1) + dot(up_grad[...], up_w[...], 1, 1)
    mixed = mixed_ref[...]
    mixed_part, gain_grad = norm_back(mixed, inverse_rms(mixed), gains[2:3, :], ffn_in_grad)
    sums[1][...] += gain_grad
    mixed_grad = grad_rows[...].astype(F32) + mixed_part
    mixed_grad_ref[...] = mixed_grad
    branch = branch_ref[...]
    branch_grad, gain_grad = norm_back(branch, inverse_rms(branch), gains[1:2, :], mixed_grad)
    sums[0][...] += gain_grad
    branch_grad = branch_grad.astype(BF)
    branch_grad_ref[...] = branch_grad
    attended_grad_ref[...] = dot(branch_grad, wo[...], 1, 1).astype(BF)


def hidden_back_rows(tiles, fulls, weights, outs, sums):
    query_grad, key_grad, value_grad, hidden_ref, mixed_grad = tiles
    gains, wq, wk, wv = fulls
    normed_grad = (
        dot(query_grad[...], wq[...], 1, 1)
        + dot(key_grad[...], wk[...], 1, 1)
        + dot(value_grad[...], wv[...], 1, 1)
    )
    hidden = hidden_ref[...]
    hidden_part, gain_grad = norm_back(hidden, inverse_rms(hidden), gains[0:1, :], normed_grad)
    sums[0][...] += gain_grad
    outs[0][...] = (mixed_grad[...] + hidden_part).astype(BF)


def joined_back_rows(tiles, fulls, weights, outs, sums):
    (hidden_grad,) = tiles
    (adapter,) = fulls
    width = hidden_grad.shape[1]
    outs[0][...] = dot(hidden_grad[...], adapter[:width, :], 1, 1).astype(BF)
    outs[1][...] = dot(hidden_grad[...], adapter[width:, :], 1, 1).astype(BF)


def body(
    latent_state,
    prelude_embed,
    out_grad,
    piece_starts,
    w_adapter,
    w_query,
    w_key,
    w_value,
    w_out,
    w_gate,
    w_up,
    w_down,
    gain_attn_in,
    gain_attn_out,
    gain_ffn_in,
    gain_ffn_out,
    *,
    shards,
    linked,
):
    links = Links() if linked else None
    seq_count, length, width = latent_state.shape
    pairs = width // PAIR
    per_call = pairs // 4
    ticks = Ticks()

    def gather(name, pieces, split, columns=False):
        ticks.add(
            name,
            gather_task(links, pieces, split, columns) if linked else plain_gather_task(pieces),
        )

    def scatter(name, grads, split):
        ticks.add(name, scatter_task(links, grads, split) if linked else plain_scatter_task(grads))

    gains = pack_gains([gain_attn_in, gain_attn_out, gain_ffn_in, gain_ffn_out])
    gather("A", [w_adapter], False)
    gather("B", [w_query, w_key, gains], False)
    gather("V", [w_value, w_out], False)
    gather("G", [w_gate], True)
    gather("U", [w_up], True)
    gather("D", [w_down], True, columns=True)
    state = latent_state.reshape(length, width)
    embed = prelude_embed.reshape(length, width)
    grad_rows = out_grad.reshape(length, width)
    hidden_units = w_gate.shape[1]
    call = functools.partial(row_call, length=length)
    tick = ticks.tick
    bias, cosine, sine = tick(["A"], lambda: (make_bias(piece_starts, length), *rotary_tables(length)))
    tick(["A", "B"])
    tick(["A", "B", "V"])
    tick(["A", "B", "V", "G"])
    (adapter_p,) = ticks.result("A")
    hidden, adapter = tick(
        ["B", "V", "G", "U"],
        lambda: call(
            hidden_rows, "hidden", tiles=[state, embed], fulls=[], weights=[adapter_p],
            outs=[(width, F32)], keep=(0,), flops=4 * width * width,
        ),
    )
    wq_p, wk_p, gains_p = ticks.result("B")
    (gains,) = tick(
        ["V", "G", "U"],
        lambda: (jnp.stack(unpack_gains(join(gains_p), shards, gain_attn_in.shape[0])),),
    )
    wv_p, wo_p = ticks.result("V")
    normed, query_rot, key_rot, value, wq, wk, wv = tick(
        ["G", "U", "D"],
        lambda: call(
            projection_rows, "projections", tiles=[hidden, cosine, sine], fulls=[gains],
            weights=[wq_p, wk_p, wv_p], outs=[(width, BF)] * 4, keep=(0, 1, 2),
            flops=6 * width * width,
        ),
    )
    results = None
    for i, names in enumerate((["G", "U", "D"], ["G", "U", "D"], ["U", "D"], ["D"])):
        results = tick(
            names,
            lambda: attention_forward(
                bias, query_rot, key_rot, value, per_call, i * per_call, results
            ),
        )
    attended, lse = results
    (gate_p,) = ticks.result("G")
    (up_p,) = ticks.result("U")
    branch, mixed, ffn_in, gate, up_value, product, wo, gate_w, up_w = tick(
        ["D"],
        lambda: call(
            feed_in_rows, "feed_in", tiles=[attended, hidden], fulls=[gains],
            weights=[wo_p, gate_p, up_p],
            outs=[(width, F32), (width, F32), (width, BF)] + [(hidden_units, BF)] * 3,
            keep=(0, 1, 2), flops=2 * width * width + 4 * width * hidden_units,
        ),
    )
    (down_p,) = ticks.result("D")
    block_output, ffn_grad, gate_grad, up_grad, gain_four_grad = tick(
        [],
        lambda: call(
            feed_out_rows, "feed_out", tiles=[product, mixed, grad_rows, gate, up_value],
            fulls=[gains], weights=[down_p],
            outs=[(width, BF), (width, BF), (hidden_units, BF), (hidden_units, BF)], sums=1,
            flops=4 * width * hidden_units,
        ),
    )
    (down_grad,) = tick([], lambda: (matmul(product, ffn_grad, 0, 0, BF),))
    scatter("down", [down_grad], True)
    (gate_weight_grad,) = tick(["down"], lambda: (matmul(ffn_in, gate_grad, 0, 0, BF),))
    scatter("gate", [gate_weight_grad], True)
    (up_weight_grad,) = tick(["down", "gate"], lambda: (matmul(ffn_in, up_grad, 0, 0, BF),))
    scatter("up", [up_weight_grad], True)
    mixed_grad, branch_grad, attended_grad, gain_two_grad, gain_three_grad = tick(
        ["down", "gate", "up"],
        lambda: call(
            feed_back_rows, "feed_back", tiles=[gate_grad, up_grad, mixed, branch, grad_rows],
            fulls=[gains, gate_w, up_w, wo], weights=[],
            outs=[(width, F32), (width, BF), (width, BF)], sums=2,
            flops=2 * width * width + 4 * width * hidden_units,
        ),
    )
    (out_weight_grad,) = tick(["down", "gate", "up"], lambda: (matmul(attended, branch_grad, 0, 0, BF),))
    scatter("out", [out_weight_grad], False)
    results = None
    for i in range(4):
        results = tick(
            ["down", "gate", "up", "out"],
            lambda: attention_backward(
                bias, query_rot, key_rot, value, attended_grad, attended, lse, cosine, sine,
                per_call, i * per_call, results,
            ),
        )
    query_grad, key_grad, value_grad = results
    grads = tick(
        ["gate", "up", "out"],
        lambda: tuple(matmul(normed, grad, 0, 0, BF) for grad in (query_grad, key_grad, value_grad)),
    )
    scatter("qkv", list(grads), False)
    hidden_grad, gain_one_grad = tick(
        ["up", "out", "qkv"],
        lambda: call(
            hidden_back_rows, "hidden_back",
            tiles=[query_grad, key_grad, value_grad, hidden, mixed_grad],
            fulls=[gains, wq, wk, wv], weights=[], outs=[(width, BF)], sums=1,
            flops=6 * width * width,
        ),
    )

    def adapter_back():
        gain_grads = pack_gain_grads(
            [gain_one_grad, gain_two_grad, gain_three_grad, gain_four_grad], shards
        )
        adapter_grad = jnp.concatenate(
            [matmul(state, hidden_grad, 0, 0, BF), matmul(embed, hidden_grad, 0, 0, BF)], axis=0
        )
        return adapter_grad, gain_grads

    adapter_grad, gain_grads = tick(["out", "qkv"], adapter_back)
    scatter("adapter", [adapter_grad, gain_grads], False)
    state_grad, embed_grad = tick(
        ["qkv", "adapter"],
        lambda: call(
            joined_back_rows, "joined_back", tiles=[hidden_grad], fulls=[adapter], weights=[],
            outs=[(width, BF), (width, BF)], flops=4 * width * width,
        ),
    )
    while "adapter" in ticks.tasks or "qkv" in ticks.tasks:
        tick(["qkv", "adapter"])
    adapter_grad, gain_grads = ticks.result("adapter")
    gain_grads = unpack_gains(gain_grads, 1, gain_attn_in.shape[0])
    shape = (seq_count, length, width)
    return (
        block_output.reshape(shape),
        state_grad.reshape(shape),
        embed_grad.reshape(shape),
        adapter_grad,
        *ticks.result("qkv"),
        *ticks.result("out"),
        *ticks.result("gate"),
        *ticks.result("up"),
        *ticks.result("down"),
        *gain_grads,
    )


def solution(mesh):
    rows = P(("grp", "fsdp"), None, None)
    matrix = P("fsdp", None)
    vector = P("fsdp")
    in_specs = (rows,) * 3 + (P(("grp", "fsdp"), None),) + (matrix,) * 8 + (vector,) * 4
    out_specs = (rows,) * 3 + (matrix,) * 8 + (vector,) * 4
    shards = mesh.shape["fsdp"]
    linked = (mesh.shape["grp"], shards) == (4, 8)
    return jax.shard_map(
        functools.partial(body, shards=shards, linked=linked),
        mesh=mesh,
        in_specs=in_specs,
        out_specs=out_specs,
        check_vma=False,
    )
```

```python
import functools

import jax
import jax.numpy as jnp
from jax import lax
from jax.experimental import pallas as pl
from jax.experimental.pallas import tpu as pltpu
from jax.sharding import PartitionSpec as P

HEAD_DIM = 64
PIECE = 256
PAIR = 2 * HEAD_DIM
GAIN_ROWS = 8
TILE = 256
MIB = 1 << 20
SHORT = pl.CostEstimate(flops=1024, transcendentals=0, bytes_accessed=1024)

EPS = 1e-06
NEG = -1e30
THETA = 50000.0
AXES = ("grp", "fsdp")
F32 = jnp.float32
BF = jnp.bfloat16


def dot(left, right, left_dim, right_dim):
    return lax.dot_general(
        left, right, (((left_dim,), (right_dim,)), ((), ())), preferred_element_type=F32
    )


def inverse_rms(value):
    return lax.rsqrt(jnp.mean(value * value, axis=-1, keepdims=True) + EPS)


def norm_back(value, inverse, gain, grad_out):
    scaled = gain * grad_out
    unit = value * inverse
    gain_grad = jnp.sum(grad_out * unit, axis=0, keepdims=True)
    mean = jnp.mean(scaled * unit, axis=-1, keepdims=True)
    return inverse * (scaled - unit * mean), gain_grad


def bias_kernel(starts_ref, bias_ref):
    rows, length = bias_ref.shape
    key_pos = lax.broadcasted_iota(jnp.int32, (rows, length), 0) + pl.program_id(0) * rows
    query_pos = lax.broadcasted_iota(jnp.int32, (rows, length), 1)
    allowed = key_pos <= query_pos
    for k in range(2):
        first = starts_ref[0, k]
        last = first + PIECE
        allowed = allowed | (
            (key_pos >= first) & (key_pos < last) & (query_pos >= first) & (query_pos < last)
        )
    bias_ref[...] = jnp.where(allowed, 0.0, NEG).astype(BF)


def make_bias(starts, length):
    rows = 128
    return pl.pallas_call(
        bias_kernel,
        grid=(length // rows,),
        in_specs=[pl.BlockSpec(memory_space=pltpu.SMEM)],
        out_specs=pl.BlockSpec((rows, length), lambda i: (i, 0)),
        out_shape=jax.ShapeDtypeStruct((length, length), BF),
        name="bias",
    )(starts)


def swap_halves(values):
    width = values.shape[1]
    half = HEAD_DIM // 2
    lane = lax.broadcasted_iota(jnp.int32, values.shape, 1)
    return jnp.where(
        (lane % HEAD_DIM) < half,
        pltpu.roll(values, width - half, 1),
        pltpu.roll(values, half, 1),
    )


def extents(length, rows):
    slot = length // 2
    return [(lo, ((lo + rows - 1) // slot + 1) * slot) for lo in range(0, length, rows)]


def add_bias(scores, bias_ref, lo, hi, rows):
    bias = bias_ref[lo:hi, lo : lo + rows].astype(F32)
    if lo == 0:
        return scores + bias
    return jnp.concatenate([scores[:lo], scores[lo:] + bias], axis=0)


def only(array, a):
    low = lax.broadcasted_iota(jnp.int32, array.shape, 1) < HEAD_DIM
    zero = BF(0)
    return jnp.where(low, array, zero) if a == 0 else jnp.where(low, zero, array)


def forward_kernel(bias_ref, q_ref, k_ref, v_ref, o_ref, lse_ref, *, length, rows):
    query_rot = q_ref[...]
    key_rot = k_ref[...]
    value_t = v_ref[...].T
    keys = (only(key_rot, 0), only(key_rot, 1))
    for lo, hi in extents(length, rows):
        block = query_rot[lo : lo + rows]
        outs = []
        for a in range(2):
            scores = add_bias(dot(keys[a][:hi], block, 1, 1), bias_ref, lo, hi, rows)
            top = jnp.max(scores, axis=0, keepdims=True)
            exponent = jnp.exp(scores - top)
            total = jnp.sum(exponent, axis=0, keepdims=True)
            lse_ref[0, a : a + 1, lo : lo + rows] = top + jnp.log(total)
            head = value_t[HEAD_DIM * a : HEAD_DIM * (a + 1), :hi]
            outs.append(dot(head, exponent.astype(BF), 1, 0) * (1.0 / total))
        o_ref[lo : lo + rows, :] = jnp.concatenate(outs, 0).T.astype(BF)


def backward_kernel(
    bias_ref, q_ref, k_ref, v_ref, g_ref, o_ref, lse_ref, cos_ref, sin_ref,
    dq_ref, dk_ref, dv_ref, *, length, rows
):
    query_rot = q_ref[...]
    key_rot = k_ref[...]
    value = v_ref[...]
    grad = g_ref[...]
    keys = (only(key_rot, 0), only(key_rot, 1))
    values = (only(value, 0), only(value, 1))
    key_t = key_rot.T
    product = grad.astype(F32) * o_ref[...].astype(F32)
    key_grad = jnp.zeros((length, PAIR), F32)
    value_grad = jnp.zeros((length, PAIR), F32)
    cosine = cos_ref[...]
    sine = sin_ref[...]

    def turn_back(array, lo, count):
        return array * cosine[lo : lo + count] - swap_halves(array) * sine[lo : lo + count]

    def add_rows(total, part, hi):
        if hi == length:
            return total + part
        return jnp.concatenate([total[:hi] + part, total[hi:]], axis=0)

    for lo, hi in extents(length, rows):
        query_block = query_rot[lo : lo + rows]
        grad_block = grad[lo : lo + rows]
        product_t = product[lo : lo + rows].T
        parts = []
        for a in range(2):
            delta = jnp.sum(product_t[HEAD_DIM * a : HEAD_DIM * (a + 1)], axis=0, keepdims=True)
            scores = dot(keys[a][:hi], query_block, 1, 1) - lse_ref[0, a : a + 1, lo : lo + rows]
            probs = jnp.exp(add_bias(scores, bias_ref, lo, hi, rows))
            probs_grad = dot(values[a][:hi], grad_block, 1, 1)
            score_grad = (probs * (probs_grad - delta)).astype(BF)
            value_grad = add_rows(value_grad, dot(probs.astype(BF), only(grad_block, a), 1, 0), hi)
            key_grad = add_rows(key_grad, dot(score_grad, only(query_block, a), 1, 0), hi)
            parts.append(dot(key_t[HEAD_DIM * a : HEAD_DIM * (a + 1), :hi], score_grad, 1, 0))
        query_grad = (jnp.concatenate(parts, 0) * HEAD_DIM**-0.5).T
        dq_ref[lo : lo + rows, :] = turn_back(query_grad, lo, rows).astype(BF)
    dk_ref[...] = turn_back(key_grad, 0, length).astype(BF)
    dv_ref[...] = value_grad.astype(BF)


def rotary_tables(length):
    half = HEAD_DIM // 2
    position = jnp.arange(length, dtype=F32)
    frequency = THETA ** (-jnp.arange(half, dtype=F32) / half)
    angles = position[:, None] * frequency[None, :]
    cosine, sine = jnp.cos(angles), jnp.sin(angles)
    return (
        jnp.concatenate([cosine] * 4, axis=1),
        jnp.concatenate([-sine, sine, -sine, sine], axis=1),
    )


def attention_call(kernel, name, steps, inputs, in_specs, out_specs, out_shape):
    return pl.pallas_call(
        kernel,
        grid=(steps,),
        in_specs=in_specs,
        out_specs=out_specs,
        out_shape=out_shape,
        compiler_params=pltpu.CompilerParams(vmem_limit_bytes=48 * MIB),
        cost_estimate=SHORT,
        name=name,
    )(*inputs)


def attention_specs(length, first):
    square = pl.BlockSpec((length, length), lambda i: (0, 0), pipeline_mode=pl.Buffered(1))
    column = pl.BlockSpec((length, PAIR), lambda i: (0, i + first))
    own = pl.BlockSpec((length, PAIR), lambda i: (0, i))
    table = pl.BlockSpec((length, PAIR), lambda i: (0, 0))
    sums = pl.BlockSpec((1, 2, length), lambda i: (i, 0, 0))
    return square, column, own, table, sums


def attention_forward(bias, query_rot, key_rot, value, steps, first, rows=512):
    length = query_rot.shape[0]
    square, column, own, table, sums = attention_specs(length, first)
    return attention_call(
        functools.partial(forward_kernel, length=length, rows=rows),
        "attention_forward",
        steps,
        [bias, query_rot, key_rot, value],
        [square, column, column, column],
        [own, sums],
        [
            jax.ShapeDtypeStruct((length, steps * PAIR), BF),
            jax.ShapeDtypeStruct((steps, 2, length), F32),
        ],
    )


def attention_backward(
    bias, query_rot, key_rot, value, grad, attended, lse, cosine, sine, steps, first, rows=256
):
    length = query_rot.shape[0]
    square, column, own, table, sums = attention_specs(length, first)
    return attention_call(
        functools.partial(backward_kernel, length=length, rows=rows),
        "attention_backward",
        steps,
        [bias, query_rot, key_rot, value, grad, attended, lse, cosine, sine],
        [square, column, column, column, column, own, sums, table, table],
        [own, own, own],
        [jax.ShapeDtypeStruct((length, steps * PAIR), BF)] * 3,
    )


class Links:
    X, CORE, Z1, Z3, Y = 16, 8, 2, 6, 1

    def __init__(self):
        group = lax.axis_index("grp")
        shard = lax.axis_index("fsdp")
        self.x, self.core = group // 2, group % 2
        self.z, self.y = shard // 2, shard % 2

    def place(self):
        return jnp.stack([self.z, self.y, self.core, self.x]).astype(jnp.int32)

    def swap(self, value, bits):
        return lax.ppermute(value, AXES, [(d, d ^ bits) for d in range(32)])


def take(value, start, size, axis):
    return lax.dynamic_slice_in_dim(value, start, size, axis)


class Pieces:
    def __init__(self, arrays, offset, size, shape, split, place):
        self.arrays, self.offset, self.size = arrays, offset, size
        self.shape, self.split, self.place = shape, split, place

    def copies(self, place_ref, refs, target):
        if self.place is None:
            return [(refs[0], target)]
        z, y, core, x = (place_ref[i] for i in range(4))
        part = pl.ds(self.offset, self.size)
        pairs = []
        count = len(refs) // 2
        for other_core, group in enumerate((refs[:count], refs[count:])):
            c = core ^ other_core
            for r in range(4):
                for side in range(2):
                    shard = (z ^ r) * 2 + (y ^ side)
                    for k in range(2):
                        if self.split:
                            source, half = group[k].at[side, r, part], x ^ k
                        else:
                            source, half = group[side].at[r, k, part], k
                        start = (shard * 4 + 2 * c + half) * self.size
                        spot = target.at[pl.ds(pl.multiple_of(start, 8), self.size), :]
                        pairs.append((source, spot))
        return pairs


def row_call(kernel, name, length, tiles, fulls, weights, outs, sums=0, keep=(), flops=0):
    places = [w.place for w in weights if w.place is not None]
    scalars = places[:1]
    anywhere = pl.BlockSpec(memory_space=pl.ANY)
    arrays = []
    spans = []
    for weight in weights:
        known = [i for i, span in enumerate(spans) if arrays[span[0]] is weight.arrays[0]]
        if known:
            spans.append(spans[known[0]])
        else:
            spans.append((len(arrays), len(arrays) + len(weight.arrays)))
            arrays += weight.arrays
    total = sum(32 if w.place is not None else 1 for w in weights)
    steps = length // TILE

    def run(*refs):
        refs = list(refs)

        def pull(count):
            taken = refs[:count]
            del refs[:count]
            return taken

        place_ref = pull(len(scalars))
        tile_refs, full_refs, array_refs = pull(len(tiles)), pull(len(fulls)), pull(len(arrays))
        out_refs, sum_refs, keep_refs = pull(len(outs)), pull(sums), pull(len(keep))
        weight_refs = pull(len(weights))
        load_sems, keep_sems = pull(2) if weights else (None, None)
        step = pl.program_id(0)

        def kept(i):
            return pltpu.make_async_copy(weight_refs[keep[i]], keep_refs[i], keep_sems.at[i])

        if weights:

            @pl.when(step == 0)
            def _():
                loads = []
                for weight, (lo, hi), target in zip(weights, spans, weight_refs):
                    where = place_ref[0] if place_ref else None
                    for source, spot in weight.copies(where, array_refs[lo:hi], target):
                        loads.append(pltpu.make_async_copy(source, spot, load_sems.at[len(loads)]))
                        loads[-1].start()
                for load in loads:
                    load.wait()
                for i in range(len(keep)):
                    kept(i).start()

        if sums:

            @pl.when(step == 0)
            def _():
                for ref in sum_refs:
                    ref[...] = jnp.zeros_like(ref)

        kernel(tile_refs, full_refs, weight_refs, out_refs, sum_refs)
        if keep:

            @pl.when(step == steps - 1)
            def _():
                for i in range(len(keep)):
                    kept(i).wait()

    def whole(array):
        return pl.BlockSpec(array.shape, lambda i: (0, 0), pipeline_mode=pl.Buffered(1))

    moved = sum(a.size * a.dtype.itemsize for a in list(tiles) + list(fulls) + arrays)
    return pl.pallas_call(
        run,
        grid=(steps,),
        in_specs=[pl.BlockSpec(memory_space=pltpu.SMEM)] * len(scalars)
        + [pl.BlockSpec((TILE, a.shape[1]), lambda i: (i, 0)) for a in tiles]
        + [whole(a) for a in fulls]
        + [anywhere] * len(arrays),
        out_specs=[pl.BlockSpec((TILE, n), lambda i: (i, 0)) for n, _ in outs]
        + [pl.BlockSpec((1, 1024), lambda i: (0, 0))] * sums
        + [anywhere] * len(keep),
        out_shape=[jax.ShapeDtypeStruct((length, n), kind) for n, kind in outs]
        + [jax.ShapeDtypeStruct((1, 1024), F32)] * sums
        + [jax.ShapeDtypeStruct(weights[i].shape, BF) for i in keep],
        scratch_shapes=[pltpu.VMEM(w.shape, BF) for w in weights]
        + (
            [pltpu.SemaphoreType.DMA((total,)), pltpu.SemaphoreType.DMA((max(len(keep), 1),))]
            if weights
            else []
        ),
        compiler_params=pltpu.CompilerParams(vmem_limit_bytes=56 * MIB),
        cost_estimate=SHORT,
        name=name,
    )(*scalars, *tiles, *fulls, *arrays)


def pack(links, pieces, split):
    width = pieces[0].shape[1]
    packed = [piece.reshape(4, -1, width) for piece in pieces]
    packed = packed[0] if len(packed) == 1 else jnp.concatenate(packed, axis=1)
    if split:
        return take(packed, 2 * links.core + links.x, 1, 0)[0]
    return take(packed, 2 * links.core, 2, 0)


def gather_task(links, mine, split):
    mine = yield mine
    far = links.swap(mine, links.Z3)
    near = links.swap(mine, links.Z1)
    mine, near, far = yield (mine, near, far)
    second = links.swap(far, links.Z1)
    mine, near, far, second = yield (mine, near, far, second)
    own = jnp.stack([mine, near, second, far])
    other = links.swap(own, links.Y)
    own, other = yield (own, other)
    if split:
        own = jnp.stack([own, other])
        other = links.swap(own, links.X)
        own, other = yield (own, other)
    own_twin, other_twin = links.swap(own, links.CORE), links.swap(other, links.CORE)
    yield (own, other, own_twin, other_twin)


def unpack(links, arrays, shards_of, split):
    results = []
    offset = 0
    for rows, width in shards_of:
        size = rows // 4
        results.append(Pieces(list(arrays), offset, size, (8 * rows, width), split, links.place()))
        offset += size
    return results


def scatter_task(links, grads, split):
    grads = yield grads
    columns = grads[0].shape[1]
    quarters = [grad.shape[0] // 32 for grad in grads]
    whole = [grad.reshape(8, 4, q, columns) for grad, q in zip(grads, quarters)]

    def half(which):
        parts = [take(item, 2 * which, 2, 1) for item in whole]
        return parts[0] if len(parts) == 1 else jnp.concatenate(parts, axis=2)

    got, *whole = yield (links.swap(half(1 - links.core), links.CORE), *whole)
    both = (half(links.core) + got).reshape(4, 2, 2, sum(quarters), columns)
    other = take(both, 1 - links.y, 1, 1)[:, 0]
    own = take(both, links.y, 1, 1)[:, 0]
    if split:
        got = links.swap(take(other, 1 - links.x, 1, 1), links.X)
        own, other, got = yield (own, other, got)
        other = links.swap(take(other, links.x, 1, 1) + got, links.Y)
        own, other = yield (own, other)
        own = lax.dynamic_update_slice_in_dim(own, take(own, links.x, 1, 1) + other, links.x, 1)
    else:
        other = links.swap(other, links.Y)
        own, other = yield (own, other)
        own = own + other

    def at(bits):
        return take(own, links.z ^ bits, 1, 0)[0]

    second = links.swap(at(2), links.Z1)
    own, second = yield (own, second)
    far = links.swap(at(3) + second, links.Z3)
    near = links.swap(at(1), links.Z1)
    own, near, far = yield (own, near, far)
    total = at(0) + near + far
    got = links.swap(total, links.X)
    total, got = yield (total, got)
    total = total + got
    twin = links.swap(total, links.CORE)
    yield (total, twin)


def far_scatter_task(links, grads):
    grads = yield grads
    width = grads[0].shape[1]
    rows = grads[0].shape[0] // 8
    whole = [grad.reshape(8, 2, rows // 2, width) for grad in grads]

    def half(which):
        parts = [take(item, which, 1, 1) for item in whole]
        return parts[0] if len(parts) == 1 else jnp.concatenate(parts, axis=2)

    got, *whole = yield (links.swap(half(1 - links.core), links.CORE), *whole)
    total = (half(links.core) + got).reshape(4 * len(grads) * rows, width)
    total = yield lax.psum_scatter(total, "fsdp", scatter_dimension=0, tiled=True)
    total, got = yield (total, links.swap(total, links.X))
    total = total + got
    yield (total, links.swap(total, links.CORE))


def summed(links, arrays, rows_of, far):
    total, twin = arrays
    columns = total.shape[-1]
    results = []
    offset = 0
    for rows in rows_of:
        q = rows // 2 if far else rows // 4
        own, other = (
            item[..., offset : offset + q, :].reshape(rows // 2, columns).astype(F32)
            for item in (total, twin)
        )
        offset += q
        pair = jnp.where(links.core == 0, jnp.stack([own, other]), jnp.stack([other, own]))
        results.append(pair.reshape(rows, columns))
    return results


def pack_gains(gains):
    rows = jnp.stack(gains)
    width = 1024
    return jnp.pad(rows[:, None], ((0, 0), (0, GAIN_ROWS - 1), (0, width - rows.shape[1]))).reshape(
        4 * GAIN_ROWS, width
    )


def join_kernel(place_ref, *refs, weight):
    out, sems = refs[-2:]
    copies = []
    for source, spot in weight.copies(place_ref, refs[:-2], out):
        copies.append(pltpu.make_async_copy(source, spot, sems.at[len(copies)]))
        copies[-1].start()
    for item in copies:
        item.wait()


def join(weight):
    if weight.place is None:
        return weight.arrays[0]
    return pl.pallas_call(
        functools.partial(join_kernel, weight=weight),
        in_specs=[pl.BlockSpec(memory_space=pltpu.SMEM)]
        + [pl.BlockSpec(memory_space=pl.ANY)] * len(weight.arrays),
        out_specs=pl.BlockSpec(memory_space=pltpu.VMEM),
        out_shape=jax.ShapeDtypeStruct(weight.shape, BF),
        scratch_shapes=[pltpu.SemaphoreType.DMA((32,))],
        name="join",
    )(weight.place, *weight.arrays)


def unpack_gains(rows, shards, size):
    rows = rows.reshape(shards, 4, GAIN_ROWS, -1)[:, :, 0, :size]
    return [rows[:, j].reshape(shards * size).astype(F32) for j in range(4)]


def pack_gain_grads(grads, shards):
    rows = jnp.stack([grad.reshape(shards, -1) for grad in grads], axis=1).astype(BF)
    return jnp.pad(
        rows[:, :, None], ((0, 0), (0, 0), (0, GAIN_ROWS - 1), (0, 1024 - rows.shape[2]))
    ).reshape(shards * 4 * GAIN_ROWS, 1024)


def matmul(left, right, left_dim, right_dim, kind=F32):
    return dot(left, right, left_dim, right_dim).astype(kind)


def chunks(size):
    step = next(n for n in (256, 128) if size % n == 0)
    return [(lo, lo + step) for lo in range(0, size, step)]


def hidden_rows(tiles, fulls, weights, outs, sums):
    state, embed = tiles
    (adapter,) = weights
    width = state.shape[1]
    outs[0][...] = dot(state[...], adapter[:width, :], 1, 0) + dot(
        embed[...], adapter[width:, :], 1, 0
    )


def projection_rows(tiles, fulls, weights, outs, sums):
    hidden_ref, cos_ref, sin_ref = tiles
    (gains,) = fulls
    normed_ref, query_ref, key_ref, value_ref = outs
    hidden = hidden_ref[...]
    normed = (hidden * inverse_rms(hidden) * gains[0:1, :]).astype(BF)
    normed_ref[...] = normed
    cosine, sine = cos_ref[...], sin_ref[...]
    for weight, out, scale in ((weights[0], query_ref, HEAD_DIM**-0.5), (weights[1], key_ref, None)):
        flat = dot(normed, weight[...], 1, 0)
        for lo in range(0, flat.shape[1], PAIR):
            part = flat[:, lo : lo + PAIR]
            turned = (part * cosine + swap_halves(part) * sine).astype(BF)
            out[:, lo : lo + PAIR] = turned if scale is None else turned * BF(scale)
    value_ref[...] = dot(normed, weights[2][...], 1, 0).astype(BF)


def feed_in_rows(tiles, fulls, weights, outs, sums):
    low, high, hidden = tiles
    (gains,) = fulls
    wo, gate_w, up_w = weights
    branch_ref, mixed_ref, ffn_in_ref, gate_ref, up_ref, product_ref = outs
    width = low.shape[1]
    branch = dot(low[...], wo[:width, :], 1, 0) + dot(high[...], wo[width:, :], 1, 0)
    branch_ref[...] = branch
    mixed = hidden[...] + branch * inverse_rms(branch) * gains[1:2, :]
    mixed_ref[...] = mixed
    ffn_in = (mixed * inverse_rms(mixed) * gains[2:3, :]).astype(BF)
    ffn_in_ref[...] = ffn_in
    for lo, hi in chunks(gate_w.shape[1]):
        gate = dot(ffn_in, gate_w[:, lo:hi], 1, 0)
        gate_ref[:, lo:hi] = gate.astype(BF)
        up_value = dot(ffn_in, up_w[:, lo:hi], 1, 0)
        up_ref[:, lo:hi] = up_value.astype(BF)
        product_ref[:, lo:hi] = (gate * jax.nn.sigmoid(gate) * up_value).astype(BF)


def feed_out_rows(tiles, fulls, weights, outs, sums):
    product, mixed, grad_rows, gate_ref, up_ref = tiles
    (gains,) = fulls
    (down_w,) = weights
    block_ref, ffn_grad_ref, gate_grad_ref, up_grad_ref = outs
    gain = gains[3:4, :]
    ffn_out = dot(product[...], down_w[...], 1, 0)
    inverse = inverse_rms(ffn_out)
    block_ref[...] = (mixed[...] + ffn_out * inverse * gain).astype(BF)
    ffn_grad, gain_grad = norm_back(ffn_out, inverse, gain, grad_rows[...].astype(F32))
    sums[0][...] += gain_grad
    ffn_grad = ffn_grad.astype(BF)
    ffn_grad_ref[...] = ffn_grad
    for lo, hi in chunks(down_w.shape[0]):
        product_grad = dot(ffn_grad, down_w[lo:hi, :], 1, 1)
        gate = gate_ref[:, lo:hi].astype(F32)
        sigmoid_gate = jax.nn.sigmoid(gate)
        silu = gate * sigmoid_gate
        up_grad_ref[:, lo:hi] = (product_grad * silu).astype(BF)
        slope = sigmoid_gate + silu * (1.0 - sigmoid_gate)
        gate_grad_ref[:, lo:hi] = (product_grad * up_ref[:, lo:hi].astype(F32) * slope).astype(BF)


def feed_back_rows(tiles, fulls, weights, outs, sums):
    gate_grad, up_grad, mixed_ref, branch_ref, grad_rows = tiles
    (gains,) = fulls
    gate_w, up_w, wo = weights
    mixed_grad_ref, branch_grad_ref, attended_grad_ref = outs
    ffn_in_grad = dot(gate_grad[...], gate_w[...], 1, 1) + dot(up_grad[...], up_w[...], 1, 1)
    mixed = mixed_ref[...]
    mixed_part, gain_grad = norm_back(mixed, inverse_rms(mixed), gains[2:3, :], ffn_in_grad)
    sums[1][...] += gain_grad
    mixed_grad = grad_rows[...].astype(F32) + mixed_part
    mixed_grad_ref[...] = mixed_grad
    branch = branch_ref[...]
    branch_grad, gain_grad = norm_back(branch, inverse_rms(branch), gains[1:2, :], mixed_grad)
    sums[0][...] += gain_grad
    branch_grad = branch_grad.astype(BF)
    branch_grad_ref[...] = branch_grad
    attended_grad_ref[...] = dot(branch_grad, wo[...], 1, 1).astype(BF)


def hidden_back_rows(tiles, fulls, weights, outs, sums):
    *grads, hidden_ref, mixed_grad = tiles
    (gains,) = fulls
    width = grads[0].shape[1]
    normed_grad = 0.0
    for i, grad in enumerate(grads):
        columns = pl.ds((i // 3) * width, width)
        normed_grad += dot(grad[...], weights[i % 3][:, columns], 1, 1)
    hidden = hidden_ref[...]
    hidden_part, gain_grad = norm_back(hidden, inverse_rms(hidden), gains[0:1, :], normed_grad)
    sums[0][...] += gain_grad
    outs[0][...] = (mixed_grad[...] + hidden_part).astype(BF)


def joined_back_rows(tiles, fulls, weights, outs, sums):
    (hidden_grad,) = tiles
    (adapter,) = weights
    width = hidden_grad.shape[1]
    outs[0][...] = dot(hidden_grad[...], adapter[:width, :], 1, 1).astype(BF)
    outs[1][...] = dot(hidden_grad[...], adapter[width:, :], 1, 1).astype(BF)


ORDER = (
    ("A0",),
    ("V0",),
    ("prep",),
    ("A1", "A0", "prep"),
    ("U0", "A0", "prep"),
    ("V1", "A0", "V0", "prep"),
    ("A2", "V0", "A1"),
    ("U1", "V0", "A1", "U0"),
    ("B0", "V0", "A1", "U0"),
    ("V2", "A1", "U0", "V1"),
    ("U2", "V1", "U1"),
    ("A3", "V1", "A2", "U1"),
    ("B1", "V1", "A2", "U1", "B0"),
    ("B2", "B1"),
    ("V3", "V2", "B1"),
    ("D0", "V3"),
    ("A4", "U2", "A3", "V3"),
    ("U3", "U2", "A3", "D0"),
    ("D1", "U2", "A3", "D0"),
    ("G0", "D0", "A4"),
    ("hidden", "D0", "A4"),
    ("B3", "B2", "D1", "hidden"),
    ("D2", "B2", "D1", "G0", "hidden"),
    ("G1", "G0", "B3"),
    ("proj", "G0", "B3"),
    ("U4", "U3", "G1", "proj"),
    ("G2", "U3", "G1", "proj"),
    ("D3", "U3", "D2", "G1", "proj"),
    ("att0", "U3", "D2", "G1", "proj"),
    ("att1", "U4", "att0"),
    ("G3", "G2", "att1"),
    ("D4", "G2", "D3", "att1"),
    ("feed_in", "D3", "G3"),
    ("feed_out", "D4", "feed_in"),
    ("GD",),
    ("d0", "GD"),
    ("GH0", "GD"),
    ("d1", "d0", "GH0"),
    ("GH1", "d0", "GH0"),
    ("h0", "GH1"),
    ("FB", "GH1"),
    ("h1", "h0", "FB"),
    ("AB0", "h0", "FB"),
    ("GQ0", "AB0"),
    ("p0", "GQ0"),
    ("AB1", "GQ0"),
    ("d2", "d1", "p0", "AB1"),
    ("p1", "d1", "p0", "AB1"),
    ("GQ1", "d1", "p0", "AB1"),
    ("q0", "GQ1"),
    ("d3", "d2", "GQ1"),
    ("HB", "d2", "GQ1"),
    ("q1", "q0", "d3", "HB"),
    ("GA", "q0", "d3", "HB"),
    ("a0", "p1", "GA"),
    ("p2", "p1", "GA"),
    ("JB", "p1", "GA"),
    ("a1", "q1", "a0", "p2", "JB"),
    ("q2", "q1", "a0", "p2", "JB"),
    ("p3", "q1", "a0", "p2", "JB"),
    ("q3", "q2"),
    ("p4", "q2", "p3"),
    ("a2", "a1", "q2", "p3"),
    ("q4", "a1", "p3", "q3"),
    ("p5", "a1", "q3", "p4"),
    ("a3", "q3", "p4", "a2"),
    ("h2", "h1", "a2", "q4", "p5"),
    ("q5", "h1", "a2", "q4", "p5"),
    ("a4", "a3", "q5"),
    ("h3", "a3", "h2", "q5"),
    ("a5", "a4", "h3"),
)
SPLIT = {"A": True, "B": False, "V": False, "G": False, "U": True, "D": True, "d": False, "h": True, "p": False, "q": False, "a": False}
PACKETS = {"A": ("adapter", "gains"), "B": ("query", "key"), "V": ("value", "out"), "G": ("gate",), "U": ("up",), "D": ("down",)}
OFFLOADED = ("d", "h")


class Plan:
    def __init__(self, links):
        self.links = links
        self.values = {}
        self.made = {}
        self.tasks = {}
        self.held = {}
        self.step = {}
        self.arrived = {}

    def fence(self, keys, gates, letter=None):
        keys = set(keys)
        letters = {letter} if letter else set()
        past = []
        for gate in gates:
            if gate in self.made:
                keys |= set(self.made[gate])
            elif self.step.get(gate[0]) == int(gate[1:]):
                letters.add(gate[0])
            elif gate in self.arrived:
                past.append(self.arrived[gate])
        values = {key: self.values[key] for key in sorted(keys)}
        held = {name: self.held[name] for name in sorted(letters) if name in self.held}
        if gates:
            values, held, _ = lax.optimization_barrier((values, held, past))
        self.values.update(values)
        self.held.update(held)

    def add(self, letter, task):
        self.tasks[letter] = task
        self.held[letter] = next(task)
        self.step[letter] = -1

    def advance(self, letter):
        self.held[letter] = self.tasks[letter].send(self.held[letter])
        self.step[letter] += 1
        self.arrived[f"{letter}{self.step[letter]}"] = self.held[letter]

    def compute(self, name, work):
        made = work(self.values)
        self.values.update(made)
        self.made[name] = tuple(made)


def body(
    latent_state,
    prelude_embed,
    out_grad,
    piece_starts,
    w_adapter,
    w_query,
    w_key,
    w_value,
    w_out,
    w_gate,
    w_up,
    w_down,
    gain_attn_in,
    gain_attn_out,
    gain_ffn_in,
    gain_ffn_out,
    *,
    shards,
    linked,
):
    links = Links() if linked else None
    seq_count, length, width = latent_state.shape
    half = width // 2
    pairs = width // PAIR // 2
    hidden_units = w_gate.shape[1]
    gain_size = gain_attn_in.shape[0]
    gains = pack_gains([gain_attn_in, gain_attn_out, gain_ffn_in, gain_ffn_out])
    parts = dict(
        adapter=w_adapter, gains=gains, query=w_query, key=w_key, value=w_value, out=w_out,
        gate=w_gate, up=w_up, down=w_down,
    )
    packets = {letter: [parts[name] for name in names] for letter, names in PACKETS.items()}
    sent = {
        "d": ["down"],
        "h": ["gate_w", "up_w"],
        "p": ["out0", "out1", "query0", "key0", "value0"],
        "q": ["query1", "key1", "value1"],
        "a": ["adapter", "gains_grad"],
    }
    plan = Plan(links)
    plan.values.update(
        state=latent_state.reshape(length, width),
        embed=prelude_embed.reshape(length, width),
        grad_rows=out_grad.reshape(length, width),
        starts=piece_starts,
    )
    call = functools.partial(row_call, length=length)

    def weights(*names):
        found = []
        for name in names:
            piece = parts[name]
            if linked:
                letter = next(key for key, own in PACKETS.items() if name in own)
                shapes = [item.shape for item in packets[letter]]
                all_of = unpack(links, plan.held[letter], shapes, SPLIT[letter])
                found.append(all_of[PACKETS[letter].index(name)])
            else:
                full = lax.all_gather(piece, "fsdp", axis=0, tiled=True)
                found.append(Pieces([full], 0, 0, full.shape, False, None))
        return found

    def prep(v):
        cosine, sine = rotary_tables(length)
        return dict(bias=make_bias(v["starts"], length), cosine=cosine, sine=sine)

    def hidden(v):
        adapter, packed = weights("adapter", "gains")
        (out,) = call(
            hidden_rows, "hidden", tiles=[v["state"], v["embed"]], fulls=[], weights=[adapter],
            outs=[(width, F32)], flops=4 * width * width,
        )
        return dict(hidden=out, gains=jnp.stack(unpack_gains(join(packed), shards, gain_size)))

    def proj(v):
        made = call(
            projection_rows, "projections", tiles=[v["hidden"], v["cosine"], v["sine"]],
            fulls=[v["gains"]], weights=weights("query", "key", "value"), outs=[(width, BF)] * 4,
            flops=6 * width * width,
        )
        return dict(zip(("normed", "query_rot", "key_rot", "value"), made))

    def attend(i, v):
        attended, lse = attention_forward(
            v["bias"], v["query_rot"], v["key_rot"], v["value"], pairs, i * pairs
        )
        return {f"attended{i}": attended, f"lse{i}": lse}

    def feed_in(v):
        made = call(
            feed_in_rows, "feed_in", tiles=[v["attended0"], v["attended1"], v["hidden"]],
            fulls=[v["gains"]], weights=weights("out", "gate", "up"),
            outs=[(width, F32), (width, F32), (width, BF)] + [(hidden_units, BF)] * 3,
            flops=2 * width * width + 4 * width * hidden_units,
        )
        return dict(zip(("branch", "mixed", "ffn_in", "gate", "up", "product"), made))

    def feed_out(v):
        made = call(
            feed_out_rows, "feed_out",
            tiles=[v["product"], v["mixed"], v["grad_rows"], v["gate"], v["up"]],
            fulls=[v["gains"]], weights=weights("down"),
            outs=[(width, BF), (width, BF), (hidden_units, BF), (hidden_units, BF)], sums=1,
            flops=4 * width * hidden_units,
        )
        return dict(zip(("block", "ffn_grad", "gate_grad", "up_grad", "gain3_grad"), made))

    def feed_back(v):
        made = call(
            feed_back_rows, "feed_back",
            tiles=[v["gate_grad"], v["up_grad"], v["mixed"], v["branch"], v["grad_rows"]],
            fulls=[v["gains"]], weights=weights("gate", "up", "out"),
            outs=[(width, F32), (width, BF), (width, BF)], sums=2,
            flops=2 * width * width + 4 * width * hidden_units,
        )
        names = ("mixed_grad", "branch_grad", "attended_grad", "gain1_grad", "gain2_grad")
        return dict(zip(names, made))

    def attend_back(i, v):
        made = attention_backward(
            v["bias"], v["query_rot"], v["key_rot"], v["value"], v["attended_grad"],
            v[f"attended{i}"], v[f"lse{i}"], v["cosine"], v["sine"], pairs, i * pairs,
        )
        return dict(zip((f"dq{i}", f"dk{i}", f"dv{i}"), made))

    def head_grads(i, v):
        made = {
            f"query{i}": matmul(v["normed"], v[f"dq{i}"], 0, 0, BF),
            f"key{i}": matmul(v["normed"], v[f"dk{i}"], 0, 0, BF),
            f"value{i}": matmul(v["normed"], v[f"dv{i}"], 0, 0, BF),
        }
        if i == 0:
            for j in range(2):
                part = v["branch_grad"][:, j * half : (j + 1) * half]
                made[f"out{j}"] = jnp.concatenate(
                    [matmul(v[f"attended{k}"], part, 0, 0, BF) for k in range(2)], axis=0
                )
        return made

    def hidden_back(v):
        made = call(
            hidden_back_rows, "hidden_back",
            tiles=[v[f"d{n}{i}"] for i in range(2) for n in "qkv"] + [v["hidden"], v["mixed_grad"]],
            fulls=[v["gains"]], weights=weights("query", "key", "value"), outs=[(width, BF)], sums=1,
            flops=6 * width * width,
        )
        return dict(zip(("hidden_grad", "gain0_grad"), made))

    def adapter_back(v):
        grad = v["hidden_grad"]
        adapter = jnp.concatenate(
            [matmul(v["state"], grad, 0, 0, BF), matmul(v["embed"], grad, 0, 0, BF)], axis=0
        )
        gain_grads = pack_gain_grads([v[f"gain{i}_grad"] for i in range(4)], shards)
        return dict(adapter=adapter, gains_grad=gain_grads)

    def joined_back(v):
        made = call(
            joined_back_rows, "joined_back", tiles=[v["hidden_grad"]], fulls=[],
            weights=weights("adapter"), outs=[(width, BF), (width, BF)], flops=4 * width * width,
        )
        return dict(zip(("state_grad", "embed_grad"), made))

    work = {
        "prep": ("starts", prep),
        "hidden": ("state", hidden),
        "proj": ("hidden", proj),
        "att0": ("query_rot", functools.partial(attend, 0)),
        "att1": ("query_rot", functools.partial(attend, 1)),
        "feed_in": ("attended1", feed_in),
        "feed_out": ("product", feed_out),
        "GD": ("ffn_grad", lambda v: dict(down=matmul(v["product"], v["ffn_grad"], 0, 0, BF))),
        "GH0": ("gate_grad", lambda v: dict(gate_w=matmul(v["ffn_in"], v["gate_grad"], 0, 0, BF))),
        "GH1": ("up_grad", lambda v: dict(up_w=matmul(v["ffn_in"], v["up_grad"], 0, 0, BF))),
        "FB": ("gate_grad", feed_back),
        "AB0": ("attended_grad", functools.partial(attend_back, 0)),
        "AB1": ("attended_grad", functools.partial(attend_back, 1)),
        "GQ0": ("dq0", functools.partial(head_grads, 0)),
        "GQ1": ("dq1", functools.partial(head_grads, 1)),
        "HB": ("dq1", hidden_back),
        "GA": ("hidden_grad", adapter_back),
        "JB": ("hidden_grad", joined_back),
    }
    if linked:
        for letter, pieces in packets.items():
            plan.add(letter, gather_task(links, pack(links, pieces, SPLIT[letter]), SPLIT[letter]))
    for name, *gates in ORDER:
        if name in work:
            key, what = work[name]
            plan.fence([key], gates)
            plan.compute(name, what)
        elif linked:
            letter = name[0]
            if letter in sent and letter not in plan.tasks:
                plan.fence(sent[letter], gates)
                grads = [plan.values[key] for key in sent[letter]]
                if letter in OFFLOADED:
                    plan.add(letter, far_scatter_task(links, grads))
                else:
                    plan.add(letter, scatter_task(links, grads, SPLIT[letter]))
            else:
                plan.fence([], gates, letter)
            plan.advance(letter)

    v = plan.values
    result = {}
    for letter, names in sent.items():
        grads = [v[name] for name in names]
        rows_of = [grad.shape[0] // shards for grad in grads]
        if linked:
            sums = summed(links, plan.held[letter], rows_of, letter in OFFLOADED)
        else:
            sums = [
                lax.psum(
                    lax.psum_scatter(grad, "fsdp", scatter_dimension=0, tiled=True), "grp"
                ).astype(F32)
                for grad in grads
            ]
        result.update(zip(names, sums))
    shape = (seq_count, length, width)

    def halves(name):
        return jnp.concatenate([result[f"{name}0"], result[f"{name}1"]], axis=1)

    return (
        v["block"].reshape(shape),
        v["state_grad"].reshape(shape),
        v["embed_grad"].reshape(shape),
        result["adapter"],
        halves("query"),
        halves("key"),
        halves("value"),
        halves("out"),
        result["gate_w"],
        result["up_w"],
        result["down"],
        *unpack_gains(result["gains_grad"], 1, gain_size),
    )


def solution(mesh):
    rows = P(("grp", "fsdp"), None, None)
    matrix = P("fsdp", None)
    vector = P("fsdp")
    in_specs = (rows,) * 3 + (P(("grp", "fsdp"), None),) + (matrix,) * 8 + (vector,) * 4
    out_specs = (rows,) * 3 + (matrix,) * 8 + (vector,) * 4
    shards = mesh.shape["fsdp"]
    linked = (mesh.shape["grp"], shards) == (4, 8)
    return jax.shard_map(
        functools.partial(body, shards=shards, linked=linked),
        mesh=mesh,
        in_specs=in_specs,
        out_specs=out_specs,
        check_vma=False,
    )
```
